32 devices in a mesh: tile: 16 (over z, x, core), rep: 2 (over y).
Axes of the slice: x: 2, y: 2, z: 4, core: 2. Of those that a mesh axis runs over, the one named last changes fastest.
Arguments:
- waves: bfloat16 [2, 8192, 128], P('rep', 'tile'), may hold values from -6 to 6
- dest_tile: int32 [2, 8192, 1], P('rep', 'tile'), may hold values from 0 to 15; in each aligned block of 512 rows (0 to 511, 512 to 1023, ..., all dimensions but the last counted through in order) at most 32 rows name the same one
- pixel_bin: int32 [2, 8192], P('rep', 'tile'), may hold values from 0 to 1023
- target: float32 [2, 128, 128], P('rep', 'tile'), may hold values from -6 to 6
- conv_one: bfloat16 [3, 3, 128, 128], replicated, may hold values from -0.1875 to 0.1875
- bias_one: float32 [128], replicated, may hold values from -0.5 to 0.5
- conv_two: bfloat16 [3, 3, 128], replicated, may hold values from -0.1875 to 0.1875
- bias_two: float32 [1], replicated, may hold values from -1 to 1
Outputs:
- prediction: float32 [2, 128, 128], P('rep', 'tile')
- update_one: float32 [3, 3, 128, 128], replicated
- update_bias: float32 [128], replicated
- update_two: float32 [3, 3, 128], replicated
The draws below stay inside these ranges and needn't reach their ends.
Inputs may be any that keep to these rules, and one draw needn't show every extreme that they name: `dest_tile`: among the rows of one device, no strip is named more than 32 times, a bound that some block reaches.
All inputs are finite; a program needn't handle non-finite values.
Results may differ from the reference program's by a relative error of at most 0.0024.
The reference program's roundings to bfloat16 on the way (of `grid`, `hidden`, `error` and `slope`) count: a program that leaves them out, or rounds other values in their place, can miss the bound.
Values may be sent and summed in bfloat16 or wider, within the bound.
A program may use at most 64 MiB of HBM per device.

```python
import math
import jax
import jax.numpy as jnp
import numpy as np
from jax import lax

STEPS = 128
C1 = 128
ROWS = 512
W = 128
CAP = 32
PIX = 1024
NH = 128
N_TILE = 16
N_REP = 2


def with_ends(drawn, rng, least, top_value):
    place = [jax.random.randint(jax.random.fold_in(rng, axis), (), 0, length) for axis, length in enumerate(drawn.shape)]
    longest = drawn.shape.index(max(drawn.shape))
    next_to = place[:longest] + [(place[longest] + 1) % drawn.shape[longest]] + place[longest + 1:]
    return drawn.at[tuple(place)].set(least).at[tuple(next_to)].set(top_value)


def block_scale(key, dims, pieces, low, largest):
    gain, own = 1.0, jax.random.fold_in(key, 6)
    for axis_at, blocks in pieces:
        draws = jnp.exp(jax.random.uniform(jax.random.fold_in(own, axis_at), (blocks,), jnp.float32, low / len(pieces), largest / len(pieces)))
        gain = gain * jnp.repeat(draws, dims[axis_at] // blocks).reshape([-1 if axis == axis_at else 1 for axis in range(len(dims))])
    return gain


def shared_out(rng, own, number, rows, amount, top, most, skew):
    sequence = jax.random.permutation(rng, amount)
    heavy_load, ordinary = shares(amount, rows * top, most, skew, True), shares(amount, rows * top, most, skew, False)
    places = jnp.arange(amount)

    def named(lengths, turn):
        used = int((lengths > 0).sum())
        fixed = max(1, used // 4)
        moved = fixed + (places - fixed + turn * (used - fixed)) % max(1, amount - fixed)
        return jnp.zeros((amount,), jnp.int32).at[sequence[jnp.where(places < fixed, places, moved)]].set(jnp.asarray(lengths, jnp.int32))

    lengths = jnp.where(number % 4 == 0, named(heavy_load, number // 4), named(ordinary, number - number // 4 - 1))
    mixed = jax.random.permutation(jax.random.fold_in(own, 3), amount)
    source_of, taker = mixed[0:amount // 2 * 2:2], mixed[1:amount // 2 * 2:2]
    slack = jnp.minimum(lengths[source_of] - 1, most - lengths[taker]) // 2
    slack = jnp.where((source_of == sequence[0]) | (taker == sequence[0]) | (lengths[taker] == 0), 0, jnp.maximum(slack, 0))
    moved = jax.random.randint(jax.random.fold_in(own, 4), (amount // 2,), 0, 1 << 20) % (slack + 1)
    lengths = lengths.at[source_of].add(-moved).at[taker].add(moved)
    members = jnp.searchsorted(jnp.cumsum(lengths), jnp.arange(rows * top), side="right").astype(jnp.int32)
    listing = members.reshape(top, rows).T
    listing = listing[jax.random.permutation(jax.random.fold_in(own, 1), rows)]
    turn = jax.random.randint(jax.random.fold_in(own, 2), (rows, 1), 0, top)
    return jnp.take_along_axis(listing, (jnp.arange(top)[None, :] + turn) % top, axis=1)


def shares(count, total, most, skew, full):
    portions = [(1 << 20) // math.isqrt(rank ** skew) + 1 for rank in range(1, count + 1)]
    largest = most if full else min(most, max(-(-total // count), total * portions[0] // sum(portions)))
    least = 1 if total - largest >= count - 1 else 0
    counts, surplus = [largest] + [least] * (count - 1), total - largest - least * (count - 1)
    while surplus > 0:
        candidates = [i for i in range(1, count) if counts[i] < largest] or [i for i in range(1, count) if counts[i] < most]
        mass, remaining = sum([portions[i] for i in candidates]), surplus
        for i in candidates:
            extra = min(most - counts[i], max(1, remaining * portions[i] // mass), surplus)
            counts[i] = counts[i] + extra
            surplus = surplus - extra
    return np.array(counts)


def scatter_about(key, shape, deviation, most, split=(), dtype=jnp.bfloat16):
    values = jax.random.normal(key, shape, jnp.float32) * deviation
    if len(split) > 0:
        values = block_scale(key, shape, split, -0.22, 0.18) * values
    return jnp.clip(values, min=-most, max=most).astype(dtype)


def setup_inputs(seed: int = 0) -> dict:
    key_list = jax.random.split(jax.random.key(seed), 9)
    waves = scatter_about(key_list[0], (N_REP, N_TILE * ROWS, STEPS), 1.0, 6.0, ((0, 2), (1, 16)))
    dest_tile_keys = jax.random.split(jax.random.fold_in(key_list[1], 1), N_REP * (N_TILE * ROWS) // ROWS)
    dest_tile_turns = jax.random.permutation(jax.random.fold_in(key_list[1], 3), N_REP * (N_TILE * ROWS) // ROWS)
    dest_tile = jax.vmap(lambda own, number: shared_out(jax.random.fold_in(key_list[1], 2), own, number, ROWS, N_TILE, 1, CAP, 2))(dest_tile_keys, dest_tile_turns).reshape((N_REP, N_TILE * ROWS, 1))
    pixel_bin = with_ends(jax.random.randint(key_list[2], (N_REP, N_TILE * ROWS), 0, PIX), jax.random.fold_in(key_list[2], 1), 0, PIX - 1).astype(jnp.int32)
    target = scatter_about(key_list[3], (N_REP, NH, W), 1.0, 6.0, ((0, 2), (1, 16)), jnp.float32)
    conv_one = scatter_about(key_list[4], (3, 3, STEPS, C1), (9 * STEPS) ** -0.5, 0.1875)
    bias_one = jnp.clip(jax.random.uniform(key_list[5], (C1,), jnp.float32, -0.5, 0.5), -0.5, 0.5)
    conv_two = scatter_about(key_list[6], (3, 3, C1), (9 * C1) ** -0.5, 0.1875)
    bias_two = jnp.clip(jax.random.uniform(key_list[7], (1,), jnp.float32, -1.0, 1.0), -1.0, 1.0)
    return {"waves": waves, "dest_tile": dest_tile, "pixel_bin": pixel_bin, "target": target, "conv_one": conv_one, "bias_one": bias_one, "conv_two": conv_two, "bias_two": bias_two}


def replica_terms(wave_rows, dest_rows, bin_rows, target_map, conv_one, bias_one, conv_two, bias_two):
    ids = dest_rows[:, 0] * PIX + bin_rows
    grid = jax.ops.segment_sum(wave_rows.astype(jnp.float32), ids, num_segments=N_TILE * PIX)
    grid = grid.astype(jnp.bfloat16).reshape(NH, W, STEPS)
    padded = jnp.pad(grid, ((2, 2), (2, 2), (0, 0)))
    pre = jnp.zeros((NH * W, C1), jnp.float32) + bias_one[None, :]
    for i in range(3):
        for j in range(3):
            patch = padded[2 * i:2 * i + NH, 2 * j:2 * j + W, :].reshape(NH * W, STEPS)
            pre = pre + jnp.dot(patch, conv_one[i, j], preferred_element_type=jnp.float32)
    pre = pre.reshape(NH, W, C1)
    hidden = jax.nn.silu(pre).astype(jnp.bfloat16)
    hidden_pad = jnp.pad(hidden, ((1, 1), (1, 1), (0, 0)))
    pred = jnp.zeros((NH, W), jnp.float32) + bias_two[0]
    for i in range(3):
        for j in range(3):
            pred = pred + jnp.einsum('hwc,c->hw', hidden_pad[i:i + NH, j:j + W, :].astype(jnp.float32), conv_two[i, j].astype(jnp.float32))
    error = ((pred - target_map) / N_REP).astype(jnp.bfloat16)
    error_pad = jnp.pad(error, ((1, 1), (1, 1)))
    grad_two = []
    back = jnp.zeros((NH, W, C1), jnp.float32)
    for i in range(3):
        for j in range(3):
            grad_two.append(jnp.einsum('hwc,hw->c', hidden_pad[i:i + NH, j:j + W, :].astype(jnp.float32), error.astype(jnp.float32)))
            shifted = error_pad[2 - i:2 - i + NH, 2 - j:2 - j + W].astype(jnp.float32)
            back = back + shifted[:, :, None] * conv_two[i, j].astype(jnp.float32)[None, None, :]
    grad_two = jnp.stack(grad_two).reshape(3, 3, C1)
    sig = jax.nn.sigmoid(pre)
    slope = (back * sig * (1.0 + pre * (1.0 - sig))).astype(jnp.bfloat16)
    slope_flat = slope.reshape(NH * W, C1)
    grad_one = []
    for i in range(3):
        for j in range(3):
            patch = padded[2 * i:2 * i + NH, 2 * j:2 * j + W, :].reshape(NH * W, STEPS)
            grad_one.append(lax.dot_general(patch, slope_flat, (((0,), (0,)), ((), ())), preferred_element_type=jnp.float32))
    grad_one = jnp.stack(grad_one).reshape(3, 3, STEPS, C1)
    grad_bias = lax.optimization_barrier(jnp.sum(slope_flat.astype(jnp.float32), axis=0))
    return (pred, grad_one, grad_bias, grad_two)

def normalized(grad):
    return grad / jnp.sqrt(jnp.mean(grad * grad) + 1e-06)

def reference(waves, dest_tile, pixel_bin, target, conv_one, bias_one, conv_two, bias_two):
    preds = []
    total_one = jnp.zeros((3, 3, STEPS, C1), jnp.float32)
    total_bias = jnp.zeros((C1,), jnp.float32)
    total_two = jnp.zeros((3, 3, C1), jnp.float32)
    for r in range(N_REP):
        pred, grad_one, grad_bias, grad_two = replica_terms(waves[r], dest_tile[r], pixel_bin[r], target[r], conv_one, bias_one, conv_two, bias_two)
        preds.append(pred)
        total_one = total_one + grad_one
        total_bias = total_bias + grad_bias
        total_two = total_two + grad_two
    return (jnp.stack(preds), normalized(total_one), normalized(total_bias), normalized(total_two))
```

```python
import functools

import jax
import jax.numpy as jnp
from jax import lax
from jax.experimental import pallas as pl
from jax.experimental.pallas import tpu as pltpu
from jax.sharding import PartitionSpec as P

CAP = 32
HALO = 4
MESH = pl.DeviceIdType.MESH
F32 = jnp.float32
BF16 = jnp.bfloat16


def iota(shape, dim):
    return lax.broadcasted_iota(jnp.int32, shape, dim)


def dot(a, b, dims=((1,), (0,))):
    return lax.dot_general(a, b, (dims, ((), ())), preferred_element_type=F32)


def step_kernel(
    tiles, reps, part,
    dest_ref, bin_ref, waves_ref, target_ref, w1_ref, b1_ref, w2_ref, b2_ref,
    pred_ref, u1_ref, ub_ref, u2_ref,
    sendw, sendb, recvw, recvb, grid, wide, pre_s, hid_s, tlow, thigh, w2_s, taps, etap,
    full, pair, total, recvs, gathered, flat,
    aw_send, aw_recv, ab_send, ab_recv, t_send, t_recv, g_send, g_recv,
    p_send, p_recv, r_send, r_recv, n_send, n_recv, f_send, f_recv,
):
    me = lax.axis_index("tile")
    rep = lax.axis_index("rep")
    rows, steps = waves_ref.shape
    height, width = target_ref.shape
    channels = b1_ref.shape[1]
    half = tiles // 2
    groups = half * reps
    core = lax.rem(me, 2)
    partner = me + 1 - 2 * core
    chip = rep * half + me // 2
    pixels = height * width
    tall = height + HALO

    def tile_peer(k):
        return lax.rem(me + k, tiles)

    def group_peer(k):
        q = lax.rem(chip + k, groups)
        return q, {"tile": 2 * lax.rem(q, half) + core, "rep": q // half}

    barrier = pltpu.get_barrier_semaphore()

    def greet(k, carry):
        pl.semaphore_signal(barrier, inc=1, device_id={"tile": tile_peer(k), "rep": rep}, device_id_type=MESH)
        return carry

    lax.fori_loop(1, tiles, greet, 0)

    def greet_far(k, carry):
        pl.semaphore_signal(
            barrier,
            inc=1,
            device_id={"tile": 2 * lax.rem(k, half) + core, "rep": lax.rem(rep + 1 + k // half, reps)},
            device_id_type=MESH,
        )
        return carry

    lax.fori_loop(0, (reps - 1) * half, greet_far, 0)

    hits = (iota((tiles, rows), 0) == dest_ref[...]).astype(F32)
    earlier = (iota((rows, rows), 0) < iota((rows, rows), 1)).astype(F32).astype(BF16)
    ranks = dot(hits.astype(BF16), earlier)
    rank = jnp.sum(hits * ranks, axis=0, keepdims=True)
    slot = jnp.sum(hits * (ranks + (CAP * iota((tiles, rows), 0)).astype(F32)), axis=0, keepdims=True)
    place = (iota((tiles * CAP, rows), 0).astype(F32) == slot).astype(F32).astype(BF16)
    sendw[...] = dot(place, waves_ref[...]).astype(BF16)
    lane = rank + (CAP * lax.rem(me, 4)).astype(F32)
    lanes = (iota((128, rows), 0).astype(F32) == lane).astype(F32).astype(BF16)
    bins = bin_ref[...]
    high = (bins // 32).astype(F32)
    low = (bins - 32 * (bins // 32)).astype(F32)
    named = 32.0 * dot((hits * high).astype(BF16), lanes, ((1,), (1,))) + dot(
        (hits * low).astype(BF16), lanes, ((1,), (1,))
    )
    for t in range(tiles):
        sendb[t] = named[t : t + 1, :]

    pl.semaphore_wait(barrier, tiles - 1 + (reps - 1) * half)

    def wave_copy(peer, source):
        return pltpu.make_async_remote_copy(
            src_ref=sendw.at[pl.ds(pl.multiple_of(peer * CAP, CAP), CAP)],
            dst_ref=recvw.at[pl.ds(pl.multiple_of(source * CAP, CAP), CAP)],
            send_sem=aw_send.at[peer],
            recv_sem=aw_recv.at[source],
            device_id={"tile": peer, "rep": rep},
            device_id_type=MESH,
        )

    def bin_copy(peer, source):
        return pltpu.make_async_remote_copy(
            src_ref=sendb.at[peer],
            dst_ref=recvb.at[source],
            send_sem=ab_send.at[peer],
            recv_sem=ab_recv.at[source],
            device_id={"tile": peer, "rep": rep},
            device_id_type=MESH,
        )

    def scatter(k, carry):
        peer = tile_peer(k)
        wave_copy(peer, me).start()
        bin_copy(peer, me).start()
        return carry

    lax.fori_loop(1, tiles, scatter, 0)

    up = jnp.minimum(me + 1, tiles - 1)
    down = jnp.maximum(me - 1, 0)
    span = HALO * width

    def target_copy(peer, dst, k):
        return pltpu.make_async_remote_copy(
            src_ref=target_ref, dst_ref=dst, send_sem=t_send.at[k], recv_sem=t_recv.at[k],
            device_id={"tile": peer, "rep": rep}, device_id_type=MESH,
        )

    def halo_copy(peer, src, dst, k):
        return pltpu.make_async_remote_copy(
            src_ref=grid.at[pl.ds(src, span)], dst_ref=grid.at[pl.ds(dst, span)],
            send_sem=g_send.at[k], recv_sem=g_recv.at[k],
            device_id={"tile": peer, "rep": rep}, device_id_type=MESH,
        )

    to_up = target_copy(up, tlow, 0)
    to_down = target_copy(down, thigh, 1)
    grid_up = halo_copy(up, span + pixels - span, 0, 0)
    grid_down = halo_copy(down, span, span + pixels, 1)
    has_up = me < tiles - 1
    has_down = me > 0

    @pl.when(has_up)
    def _():
        to_up.start()

    @pl.when(has_down)
    def _():
        to_down.start()

    @pl.when(jnp.logical_not(has_down))
    def _():
        grid[0:span, :] = jnp.zeros((span, steps), BF16)
        tlow[...] = jnp.zeros((height, width), F32)

    @pl.when(jnp.logical_not(has_up))
    def _():
        grid[span + pixels : span + pixels + span, :] = jnp.zeros((span, steps), BF16)
        thigh[...] = jnp.zeros((height, width), F32)

    own = pl.ds(pl.multiple_of(me * CAP, CAP), CAP)
    recvw[own, :] = sendw[own, :]
    recvb[me] = sendb[me]
    w2_s[...] = jnp.zeros(w2_s.shape, F32)
    for i in range(3):
        w2_s[8 * i : 8 * i + 3, :] = w2_ref[i].astype(F32)
    w2 = w2_s[...].astype(BF16)

    def arrive(k, carry):
        peer = tile_peer(k)
        wave_copy(peer, peer).wait_recv()
        bin_copy(peer, peer).wait_recv()
        return carry

    lax.fori_loop(1, tiles, arrive, 0)

    names = []
    for q in range(tiles // 4):
        names.append(recvb[4 * q] + recvb[4 * q + 1] + recvb[4 * q + 2] + recvb[4 * q + 3])
    names = jnp.concatenate(names, axis=1)
    block = 256
    order = [0, pixels - block] + [s for s in range(block, pixels - block, block)]
    for start in order:
        wanted = (iota((block, tiles * CAP), 0) + start).astype(F32)
        onehot = (wanted == names).astype(F32).astype(BF16)
        grid[span + start : span + start + block, :] = dot(onehot, recvw[...]).astype(BF16)

    @pl.when(has_up)
    def _():
        grid_up.start()

    @pl.when(has_down)
    def _():
        grid_down.start()

    column = iota((width, steps), 0)

    def spread(y):
        line = grid[y * width : (y + 1) * width, :]
        value = line.astype(F32)
        left = jnp.where(column >= 2, pltpu.roll(value, 2, 0), 0.0)
        right = jnp.where(column < width - 2, pltpu.roll(value, width - 2, 0), 0.0)
        wide[y * width : (y + 1) * width, 0:steps] = left.astype(BF16)
        wide[y * width : (y + 1) * width, steps : 2 * steps] = line
        wide[y * width : (y + 1) * width, 2 * steps : 3 * steps] = right.astype(BF16)

    for y in range(HALO, HALO + height):
        spread(y)

    @pl.when(has_down)
    def _():
        grid_up.wait_recv()

    @pl.when(has_up)
    def _():
        grid_down.wait_recv()

    for y in list(range(HALO)) + list(range(HALO + height, 2 * HALO + height)):
        spread(y)

    bias = b1_ref[...]
    for y in range(0, tall, 2):
        acc = jnp.zeros((2 * width, channels), F32) + bias
        for i in range(3):
            acc = acc + dot(wide[(y + 2 * i) * width : (y + 2 * i + 2) * width, :], w1_ref[i])
        sig = 1.0 / (1.0 + jnp.exp(-acc))
        hidden = acc * sig
        if y < 2:
            hidden = jnp.where(has_down, hidden, 0.0)
        if y >= height + 2:
            hidden = jnp.where(has_up, hidden, 0.0)
        hid_s[y * width : (y + 2) * width, :] = hidden.astype(BF16)
        if 2 <= y < height + 2:
            pre_s[(y - 2) * width : y * width, :] = sig * (1.0 + acc * (1.0 - sig))

    each = dot(w2, hid_s[...], ((1,), (1,)))
    span2 = (height + 2) * width
    summed = each[0:8, 0:span2] + each[8:16, width : width + span2] + each[16:24, 2 * width : 2 * width + span2]
    taps[...] = jnp.zeros(taps.shape, F32)
    for y in range(height + 2):
        for j in range(3):
            taps[j, y : y + 1, :] = summed[j : j + 1, y * width : (y + 1) * width]
    tp = taps.shape[1]
    x_at = iota((tp, width), 1)
    y_at = iota((tp, width), 0)
    pred = (
        b2_ref[0]
        + jnp.where(x_at >= 1, pltpu.roll(taps[0], 1, 1), 0.0)
        + taps[1]
        + jnp.where(x_at < width - 1, pltpu.roll(taps[2], width - 1, 1), 0.0)
    )

    @pl.when(has_down)
    def _():
        to_up.wait_recv()

    @pl.when(has_up)
    def _():
        to_down.wait_recv()

    taps[3] = pred
    pred_ref[...] = taps[3, 1 : 1 + height, :]
    taps[4, 0:1, :] = tlow[height - 1 : height, :]
    taps[4, 1 : 1 + height, :] = target_ref[...]
    taps[4, 1 + height : 2 + height, :] = thigh[0:1, :]
    inside = jnp.logical_and(
        jnp.logical_or(y_at >= 1, has_down),
        jnp.logical_and(y_at < height + 2, jnp.logical_or(y_at < height + 1, has_up)),
    )
    error = jnp.where(inside, (pred - taps[4]) / reps, 0.0).astype(BF16).astype(F32)
    taps[0] = jnp.where(x_at < width - 1, pltpu.roll(error, width - 1, 1), 0.0)
    taps[1] = error
    taps[2] = jnp.where(x_at >= 1, pltpu.roll(error, 1, 1), 0.0)
    etap[...] = jnp.zeros(etap.shape, F32)
    for i in range(3):
        for j in range(3):
            for y in range(height):
                etap[8 * i + j : 8 * i + j + 1, y * width : (y + 1) * width] = taps[j, y + 2 - i : y + 3 - i, :]
    errors = etap[...].astype(BF16)

    mine = hid_s[2 * width : 2 * width + pixels, :]
    grad_two = dot(errors, mine)
    back = dot(errors, w2, ((0,), (0,)))
    slope = (back * pre_s[...]).astype(BF16)
    grad_bias = dot(jnp.ones((8, pixels), BF16), slope)
    piece = steps // 2
    small = 9 * piece
    for h in range(2):
        full[h, small : small + 24, :] = grad_two
        full[h, small + 24 : small + 32, :] = grad_bias
        if full.shape[1] > small + 32:
            full[h, small + 32 :, :] = jnp.zeros((full.shape[1] - small - 32, channels), F32)
    for i in range(3):
        start = (2 + 2 * i) * width
        g = dot(wide[start : start + pixels, :], slope, ((0,), (0,)))
        for j in range(3):
            k = 3 * i + j
            for h in range(2):
                full[h, k * piece : (k + 1) * piece, :] = g[j * steps + h * piece : j * steps + (h + 1) * piece, :]

    swap = pltpu.make_async_remote_copy(
        src_ref=full.at[1 - core], dst_ref=pair, send_sem=p_send, recv_sem=p_recv,
        device_id={"tile": partner, "rep": rep}, device_id_type=MESH,
    )
    swap.start()
    swap.wait_recv()
    total[...] = full[core] + pair[...]

    def share_copy(q, device, source):
        return pltpu.make_async_remote_copy(
            src_ref=total.at[pl.ds(pl.multiple_of(q * part, 8), part)], dst_ref=recvs.at[source],
            send_sem=r_send.at[q], recv_sem=r_recv.at[source], device_id=device, device_id_type=MESH,
        )

    def give(k, carry):
        q, device = group_peer(k)
        share_copy(q, device, chip).start()
        return carry

    lax.fori_loop(1, groups, give, 0)
    recvs[chip] = total[pl.ds(pl.multiple_of(chip * part, 8), part), :]

    def take(k, carry):
        q, device = group_peer(k)
        share_copy(q, device, q).wait_recv()
        return carry

    lax.fori_loop(1, groups, take, 0)
    share = lax.fori_loop(1, groups, lambda q, acc: acc + recvs[q], recvs[0])
    gathered[core, chip] = share.astype(BF16)

    def spread_copy(device, source):
        return pltpu.make_async_remote_copy(
            src_ref=gathered.at[core, chip], dst_ref=gathered.at[core, source],
            send_sem=n_send.at[source], recv_sem=n_recv.at[source], device_id=device, device_id_type=MESH,
        )

    def spread_start(k, carry):
        q, device = group_peer(k)
        pltpu.make_async_remote_copy(
            src_ref=gathered.at[core, chip], dst_ref=gathered.at[core, chip],
            send_sem=n_send.at[q], recv_sem=n_recv.at[chip], device_id=device, device_id_type=MESH,
        ).start()
        return carry

    lax.fori_loop(1, groups, spread_start, 0)

    def forward(q, which):
        return pltpu.make_async_remote_copy(
            src_ref=gathered.at[which, q], dst_ref=gathered.at[which, q],
            send_sem=f_send.at[q], recv_sem=f_recv.at[q],
            device_id={"tile": partner, "rep": rep}, device_id_type=MESH,
        )

    forward(chip, core).start()

    def pass_on(k, carry):
        q, device = group_peer(groups - k)
        spread_copy(device, q).wait_recv()
        forward(q, core).start()
        return carry

    lax.fori_loop(1, groups, pass_on, 0)

    def finish(q, carry):
        forward(q, 1 - core).wait_recv()
        return carry

    lax.fori_loop(0, groups, finish, 0)

    def normalized(g, count, sums):
        return g / jnp.sqrt(sums / count + 1e-06)

    for h in range(2):
        flat[h] = gathered[h].astype(F32).reshape(groups * part, channels)
    one = flat[:, 0:small, :]
    scale = jnp.sqrt(jnp.sum(one * one) / (9 * steps * channels) + 1e-06)
    for k in range(9):
        for h in range(2):
            u1_ref[k // 3, k % 3, h * piece : (h + 1) * piece, :] = flat[h, k * piece : (k + 1) * piece, :] / scale
    two = flat[0, small : small + 24, :]
    two = two / jnp.sqrt(jnp.sum(two * two) / (9 * channels) + 1e-06)
    for i in range(3):
        u2_ref[i] = two[8 * i : 8 * i + 3, :]
    gb = flat[0, small + 24 : small + 25, :]
    ub_ref[...] = gb / jnp.sqrt(jnp.sum(gb * gb) / channels + 1e-06)

    @pl.when(has_up)
    def _():
        to_up.wait_send()
        grid_up.wait_send()

    @pl.when(has_down)
    def _():
        to_down.wait_send()
        grid_down.wait_send()

    def sent(k, carry):
        peer = tile_peer(k)
        wave_copy(peer, me).wait_send()
        bin_copy(peer, me).wait_send()
        return carry

    lax.fori_loop(1, tiles, sent, 0)
    swap.wait_send()

    def shared(k, carry):
        q, device = group_peer(k)
        share_copy(q, device, chip).wait_send()
        spread_copy(device, q).wait_send()
        return carry

    lax.fori_loop(1, groups, shared, 0)

    def passed(q, carry):
        forward(q, core).wait_send()
        return carry

    lax.fori_loop(0, groups, passed, 0)


def on_device(tiles, reps, waves, dest_tile, pixel_bin, target, conv_one, bias_one, conv_two, bias_two):
    rows, steps = waves.shape[1:]
    height, width = target.shape[1:]
    channels = conv_one.shape[3]
    pixels = height * width
    groups = tiles // 2 * reps
    small = 9 * (steps // 2)
    part = -(-(small + 32) // (8 * groups)) * 8
    padded = groups * part
    tp = -(-(height + 2) // 8) * 8
    dma = pltpu.SemaphoreType.DMA
    vmem = pl.BlockSpec(memory_space=pltpu.VMEM)
    pred, one, bias, two = pl.pallas_call(
        functools.partial(step_kernel, tiles, reps, part),
        out_shape=(
            jax.ShapeDtypeStruct((height, width), F32),
            jax.ShapeDtypeStruct((3, 3, steps, channels), F32),
            jax.ShapeDtypeStruct((1, channels), F32),
            jax.ShapeDtypeStruct((3, 3, channels), F32),
        ),
        in_specs=[vmem] * 7 + [pl.BlockSpec(memory_space=pltpu.SMEM)],
        out_specs=(vmem,) * 4,
        scratch_shapes=[
            pltpu.VMEM((tiles * CAP, steps), BF16),
            pltpu.VMEM((tiles, 1, 128), F32),
            pltpu.VMEM((tiles * CAP, steps), BF16),
            pltpu.VMEM((tiles, 1, 128), F32),
            pltpu.VMEM(((height + 2 * HALO) * width, steps), BF16),
            pltpu.VMEM(((height + 2 * HALO) * width, 3 * steps), BF16),
            pltpu.VMEM((pixels, channels), F32),
            pltpu.VMEM(((height + HALO) * width, channels), BF16),
            pltpu.VMEM((height, width), F32),
            pltpu.VMEM((height, width), F32),
            pltpu.VMEM((24, channels), F32),
            pltpu.VMEM((5, tp, width), F32),
            pltpu.VMEM((24, pixels), F32),
            pltpu.VMEM((2, padded, channels), F32),
            pltpu.VMEM((padded, channels), F32),
            pltpu.VMEM((padded, channels), F32),
            pltpu.VMEM((groups, part, channels), F32),
            pltpu.VMEM((2, groups, part, channels), BF16),
            pltpu.VMEM((2, padded, channels), F32),
            dma((tiles,)), dma((tiles,)), dma((tiles,)), dma((tiles,)),
            dma((2,)), dma((2,)), dma((2,)), dma((2,)),
            dma, dma,
            dma((groups,)), dma((groups,)), dma((groups,)), dma((groups,)), dma((groups,)), dma((groups,)),
        ],
        compiler_params=pltpu.CompilerParams(
            collective_id=0, has_side_effects=True, vmem_limit_bytes=40 * 1024 * 1024
        ),
        name="step",
    )(
        dest_tile.reshape(1, rows), pixel_bin, waves[0], target[0],
        conv_one.reshape(3, 3 * steps, channels), bias_one.reshape(1, channels), conv_two, bias_two,
    )
    return pred[None], one, bias[0], two


def solution(mesh):
    placed = (
        P("rep", "tile", None),
        P("rep", "tile", None),
        P("rep", "tile"),
        P("rep", "tile", None),
        P(),
        P(),
        P(),
        P(),
    )
    return jax.shard_map(
        functools.partial(on_device, mesh.shape["tile"], mesh.shape["rep"]),
        mesh=mesh,
        in_specs=placed,
        out_specs=(P("rep", "tile", None), P(), P(), P()),
        check_vma=False,
    )
```

```python
import functools

import jax
import jax.numpy as jnp
from jax import lax
from jax.experimental import pallas as pl
from jax.experimental.pallas import tpu as pltpu
from jax.sharding import PartitionSpec as P

CAP = 32
HALO = 4
MESH = pl.DeviceIdType.MESH
F32 = jnp.float32
BF16 = jnp.bfloat16


def iota(shape, dim):
    return lax.broadcasted_iota(jnp.int32, shape, dim)


def dot(a, b, dims=((1,), (0,))):
    return lax.dot_general(a, b, (dims, ((), ())), preferred_element_type=F32)


def step_kernel(
    tiles, reps, part,
    dest_hbm, bin_hbm, waves_hbm, target_hbm, w1_hbm, b1_hbm, w2_hbm, b2_hbm,
    pred_ref, out_ref,
    dest_ref, bin_ref, waves_ref, target_ref, w1_ref, b1_ref, w2_ref, b2_ref, l_sem,
    sendw, sendb, recvw, recvb, grid, wide, pre_s, hid_s, tlow, thigh, w2_s, taps, etap,
    full, pair, total, recva, recvs, gathered,
    aw_send, aw_recv, ab_send, ab_recv, t_send, t_recv, g_send, g_recv,
    p_send, p_recv, s_send, s_recv, r_send, r_recv, n_send, n_recv, f_send, f_recv,
):
    me = lax.axis_index("tile")
    rep = lax.axis_index("rep")
    rows, steps = waves_ref.shape
    height, width = target_ref.shape
    channels = b1_ref.shape[1]
    half = tiles // 2
    groups = half * reps
    outer, inner = split(tiles, reps)
    minor = outer // reps
    core = lax.rem(me, 2)
    partner = me + 1 - 2 * core
    at_outer = rep * minor + lax.rem(me // 2, minor)
    at_inner = me // 2 // minor
    chip = at_outer * inner + at_inner
    pixels = height * width
    tall = height + HALO

    def tile_peer(k):
        return lax.rem(me + k, tiles)

    def group_peer(k):
        q = lax.rem(chip + k, groups)
        return q, device_at(q // inner, lax.rem(q, inner))

    def device_at(a, b):
        return {"tile": 2 * (b * minor + lax.rem(a, minor)) + core, "rep": a // minor}

    barrier = pltpu.get_barrier_semaphore()

    def greet(k, carry):
        pl.semaphore_signal(barrier, inc=1, device_id={"tile": tile_peer(k), "rep": rep}, device_id_type=MESH)
        return carry

    lax.fori_loop(1, tiles, greet, 0)

    def greet_far(k, carry):
        pl.semaphore_signal(
            barrier,
            inc=1,
            device_id={"tile": 2 * lax.rem(k, half) + core, "rep": lax.rem(rep + 1 + k // half, reps)},
            device_id_type=MESH,
        )
        return carry

    lax.fori_loop(0, (reps - 1) * half, greet_far, 0)

    loads = [
        pltpu.make_async_copy(src, dst, l_sem.at[k])
        for k, (src, dst) in enumerate(
            [
                (dest_hbm, dest_ref), (bin_hbm, bin_ref), (waves_hbm, waves_ref), (target_hbm, target_ref),
                (w1_hbm, w1_ref), (b1_hbm, b1_ref), (w2_hbm, w2_ref), (b2_hbm, b2_ref),
            ]
        )
    ]
    for load in loads:
        load.start()
    for load in loads[:4]:
        load.wait()

    hits = (iota((tiles, rows), 0) == dest_ref[...]).astype(F32)
    earlier = (iota((rows, rows), 0) < iota((rows, rows), 1)).astype(F32).astype(BF16)
    ranks = dot(hits.astype(BF16), earlier)
    rank = jnp.sum(hits * ranks, axis=0, keepdims=True)
    slot = jnp.sum(hits * (ranks + (CAP * iota((tiles, rows), 0)).astype(F32)), axis=0, keepdims=True)
    place = (iota((tiles * CAP, rows), 0).astype(F32) == slot).astype(F32).astype(BF16)
    sendw[...] = dot(place, waves_ref[...]).astype(BF16)
    lane = rank + (CAP * lax.rem(me, 4)).astype(F32)
    lanes = (iota((128, rows), 0).astype(F32) == lane).astype(F32).astype(BF16)
    bins = bin_ref[...]
    high = (bins // 32).astype(F32)
    low = (bins - 32 * (bins // 32)).astype(F32)
    named = 32.0 * dot((hits * high).astype(BF16), lanes, ((1,), (1,))) + dot(
        (hits * low).astype(BF16), lanes, ((1,), (1,))
    )
    for t in range(tiles):
        sendb[t] = named[t : t + 1, :]

    pl.semaphore_wait(barrier, tiles - 1 + (reps - 1) * half)

    def wave_copy(peer, source):
        return pltpu.make_async_remote_copy(
            src_ref=sendw.at[pl.ds(pl.multiple_of(peer * CAP, CAP), CAP)],
            dst_ref=recvw.at[pl.ds(pl.multiple_of(source * CAP, CAP), CAP)],
            send_sem=aw_send.at[peer],
            recv_sem=aw_recv.at[source],
            device_id={"tile": peer, "rep": rep},
            device_id_type=MESH,
        )

    def bin_copy(peer, source):
        return pltpu.make_async_remote_copy(
            src_ref=sendb.at[peer],
            dst_ref=recvb.at[source],
            send_sem=ab_send.at[peer],
            recv_sem=ab_recv.at[source],
            device_id={"tile": peer, "rep": rep},
            device_id_type=MESH,
        )

    def scatter(k, carry):
        peer = tile_peer(k)
        wave_copy(peer, me).start()
        bin_copy(peer, me).start()
        return carry

    lax.fori_loop(1, tiles, scatter, 0)

    up = jnp.minimum(me + 1, tiles - 1)
    down = jnp.maximum(me - 1, 0)
    span = HALO * width

    def target_copy(peer, dst, k):
        return pltpu.make_async_remote_copy(
            src_ref=target_ref, dst_ref=dst, send_sem=t_send.at[k], recv_sem=t_recv.at[k],
            device_id={"tile": peer, "rep": rep}, device_id_type=MESH,
        )

    def halo_copy(peer, src, dst, k):
        return pltpu.make_async_remote_copy(
            src_ref=grid.at[pl.ds(src, span)], dst_ref=grid.at[pl.ds(dst, span)],
            send_sem=g_send.at[k], recv_sem=g_recv.at[k],
            device_id={"tile": peer, "rep": rep}, device_id_type=MESH,
        )

    to_up = target_copy(up, tlow, 0)
    to_down = target_copy(down, thigh, 1)
    grid_up = halo_copy(up, span + pixels - span, 0, 0)
    grid_down = halo_copy(down, span, span + pixels, 1)
    has_up = me < tiles - 1
    has_down = me > 0

    @pl.when(has_up)
    def _():
        to_up.start()

    @pl.when(has_down)
    def _():
        to_down.start()

    @pl.when(jnp.logical_not(has_down))
    def _():
        grid[0:span, :] = jnp.zeros((span, steps), BF16)
        tlow[...] = jnp.zeros((height, width), F32)

    @pl.when(jnp.logical_not(has_up))
    def _():
        grid[span + pixels : span + pixels + span, :] = jnp.zeros((span, steps), BF16)
        thigh[...] = jnp.zeros((height, width), F32)

    own = pl.ds(pl.multiple_of(me * CAP, CAP), CAP)
    recvw[own, :] = sendw[own, :]
    recvb[me] = sendb[me]
    for load in loads[4:]:
        load.wait()
    w2_s[...] = jnp.zeros(w2_s.shape, F32)
    for i in range(3):
        w2_s[8 * i : 8 * i + 3, :] = w2_ref[i].astype(F32)
    w2 = w2_s[...].astype(BF16)

    def arrive(k, carry):
        peer = tile_peer(k)
        wave_copy(peer, peer).wait_recv()
        bin_copy(peer, peer).wait_recv()
        return carry

    lax.fori_loop(1, tiles, arrive, 0)

    names = []
    for q in range(tiles // 4):
        names.append(recvb[4 * q] + recvb[4 * q + 1] + recvb[4 * q + 2] + recvb[4 * q + 3])
    names = jnp.concatenate(names, axis=1)
    block = 256
    order = [0, pixels - block] + [s for s in range(block, pixels - block, block)]
    for start in order:
        wanted = (iota((block, tiles * CAP), 0) + start).astype(F32)
        onehot = (wanted == names).astype(F32).astype(BF16)
        grid[span + start : span + start + block, :] = dot(onehot, recvw[...]).astype(BF16)

    @pl.when(has_up)
    def _():
        grid_up.start()

    @pl.when(has_down)
    def _():
        grid_down.start()

    column = iota((width, steps), 0)

    def spread(y):
        line = grid[y * width : (y + 1) * width, :]
        value = line.astype(F32)
        left = jnp.where(column >= 2, pltpu.roll(value, 2, 0), 0.0)
        right = jnp.where(column < width - 2, pltpu.roll(value, width - 2, 0), 0.0)
        wide[y * width : (y + 1) * width, 0:steps] = left.astype(BF16)
        wide[y * width : (y + 1) * width, steps : 2 * steps] = line
        wide[y * width : (y + 1) * width, 2 * steps : 3 * steps] = right.astype(BF16)

    for y in range(HALO, HALO + height):
        spread(y)

    bias = b1_ref[...]

    def convolve(y):
        acc = jnp.zeros((2 * width, channels), F32) + bias
        for i in range(3):
            acc = acc + dot(wide[(y + 2 * i) * width : (y + 2 * i + 2) * width, :], w1_ref[i])
        sig = 1.0 / (1.0 + jnp.exp(-acc))
        hidden = acc * sig
        if y < 2:
            hidden = jnp.where(has_down, hidden, 0.0)
        if y >= height + 2:
            hidden = jnp.where(has_up, hidden, 0.0)
        hid_s[y * width : (y + 2) * width, :] = hidden.astype(BF16)
        if 2 <= y < height + 2:
            pre_s[(y - 2) * width : y * width, :] = sig * (1.0 + acc * (1.0 - sig))

    middle = [y for y in range(HALO, height, 2)]
    for y in middle:
        convolve(y)

    @pl.when(has_down)
    def _():
        grid_up.wait_recv()

    @pl.when(has_up)
    def _():
        grid_down.wait_recv()

    for y in list(range(HALO)) + list(range(HALO + height, 2 * HALO + height)):
        spread(y)

    for y in range(0, tall, 2):
        if y not in middle:
            convolve(y)

    each = dot(w2, hid_s[...], ((1,), (1,)))
    span2 = (height + 2) * width
    summed = each[0:8, 0:span2] + each[8:16, width : width + span2] + each[16:24, 2 * width : 2 * width + span2]
    taps[...] = jnp.zeros(taps.shape, F32)
    for y in range(height + 2):
        for j in range(3):
            taps[j, y : y + 1, :] = summed[j : j + 1, y * width : (y + 1) * width]
    tp = taps.shape[1]
    x_at = iota((tp, width), 1)
    y_at = iota((tp, width), 0)
    pred = (
        b2_ref[0]
        + jnp.where(x_at >= 1, pltpu.roll(taps[0], 1, 1), 0.0)
        + taps[1]
        + jnp.where(x_at < width - 1, pltpu.roll(taps[2], width - 1, 1), 0.0)
    )

    @pl.when(has_down)
    def _():
        to_up.wait_recv()

    @pl.when(has_up)
    def _():
        to_down.wait_recv()

    taps[3] = pred
    pred_ref[...] = taps[3, 1 : 1 + height, :]
    taps[4, 0:1, :] = tlow[height - 1 : height, :]
    taps[4, 1 : 1 + height, :] = target_ref[...]
    taps[4, 1 + height : 2 + height, :] = thigh[0:1, :]
    inside = jnp.logical_and(
        jnp.logical_or(y_at >= 1, has_down),
        jnp.logical_and(y_at < height + 2, jnp.logical_or(y_at < height + 1, has_up)),
    )
    error = jnp.where(inside, (pred - taps[4]) / reps, 0.0).astype(BF16).astype(F32)
    taps[0] = jnp.where(x_at < width - 1, pltpu.roll(error, width - 1, 1), 0.0)
    taps[1] = error
    taps[2] = jnp.where(x_at >= 1, pltpu.roll(error, 1, 1), 0.0)
    etap[...] = jnp.zeros(etap.shape, F32)
    for i in range(3):
        for j in range(3):
            for y in range(height):
                etap[8 * i + j : 8 * i + j + 1, y * width : (y + 1) * width] = taps[j, y + 2 - i : y + 3 - i, :]
    errors = etap[...].astype(BF16)

    mine = hid_s[2 * width : 2 * width + pixels, :]
    grad_two = dot(errors, mine)
    back = dot(errors, w2, ((0,), (0,)))
    slope = (back * pre_s[...]).astype(BF16)
    grad_bias = dot(jnp.ones((8, pixels), BF16), slope)
    piece = steps // 2
    small = 9 * piece
    for h in range(2):
        full[h, small : small + 24, :] = grad_two
        full[h, small + 24 : small + 32, :] = grad_bias
        if full.shape[1] > small + 32:
            full[h, small + 32 :, :] = jnp.zeros((full.shape[1] - small - 32, channels), F32)
    slab = inner * part

    def swap(a):
        rows_a = pl.ds(a * slab, slab)
        return pltpu.make_async_remote_copy(
            src_ref=full.at[1 - core, rows_a], dst_ref=pair.at[rows_a],
            send_sem=p_send.at[a], recv_sem=p_recv.at[a],
            device_id={"tile": partner, "rep": rep}, device_id_type=MESH,
        )

    started = 0
    for i in range(3):
        start = (2 + 2 * i) * width
        g = dot(wide[start : start + pixels, :], slope, ((0,), (0,)))
        for j in range(3):
            k = 3 * i + j
            for h in range(2):
                full[h, k * piece : (k + 1) * piece, :] = g[j * steps + h * piece : j * steps + (h + 1) * piece, :]
        while started < outer and ((started + 1) * slab <= 3 * (i + 1) * piece or i == 2):
            swap(started).start()
            started += 1

    def slab_copy(a, source):
        return pltpu.make_async_remote_copy(
            src_ref=total.at[pl.ds(a * slab, slab)], dst_ref=recva.at[source],
            send_sem=s_send.at[a], recv_sem=s_recv.at[source],
            device_id=device_at(a, at_inner), device_id_type=MESH,
        )

    for a in range(outer):
        swap(a).wait_recv()
        rows_a = slice(a * slab, (a + 1) * slab)
        total[rows_a, :] = full[core, rows_a, :] + pair[rows_a, :]

        @pl.when(at_outer != a)
        def _():
            slab_copy(a, at_outer).start()

    recva[at_outer] = total[pl.ds(pl.multiple_of(at_outer * slab, 8), slab), :]
    for a in range(outer):

        @pl.when(at_outer != a)
        def _():
            slab_copy(a, a).wait_recv()

    plane = recva[0]
    for a in range(1, outer):
        plane = plane + recva[a]
    pair[0:slab, :] = plane

    def share_copy(b, source):
        return pltpu.make_async_remote_copy(
            src_ref=pair.at[pl.ds(b * part, part)], dst_ref=recvs.at[source],
            send_sem=r_send.at[b], recv_sem=r_recv.at[source],
            device_id=device_at(at_outer, b), device_id_type=MESH,
        )

    for b in range(inner):

        @pl.when(at_inner != b)
        def _():
            share_copy(b, at_inner).start()

    recvs[at_inner] = pair[pl.ds(pl.multiple_of(at_inner * part, 8), part), :]
    for b in range(inner):

        @pl.when(at_inner != b)
        def _():
            share_copy(b, b).wait_recv()

    share = recvs[0]
    for b in range(1, inner):
        share = share + recvs[b]
    rest = share - share.astype(BF16).astype(F32)
    tail = jnp.logical_and(iota(share.shape, 0) + chip * part >= small, core == 1)
    gathered[core, chip] = jnp.where(tail, rest, share).astype(BF16)

    def spread_copy(device, source):
        return pltpu.make_async_remote_copy(
            src_ref=gathered.at[core, chip], dst_ref=gathered.at[core, source],
            send_sem=n_send.at[source], recv_sem=n_recv.at[source], device_id=device, device_id_type=MESH,
        )

    def spread_start(k, carry):
        q, device = group_peer(k)
        pltpu.make_async_remote_copy(
            src_ref=gathered.at[core, chip], dst_ref=gathered.at[core, chip],
            send_sem=n_send.at[q], recv_sem=n_recv.at[chip], device_id=device, device_id_type=MESH,
        ).start()
        return carry

    lax.fori_loop(1, groups, spread_start, 0)

    def forward(q, which):
        return pltpu.make_async_remote_copy(
            src_ref=gathered.at[which, q], dst_ref=gathered.at[which, q],
            send_sem=f_send.at[q], recv_sem=f_recv.at[q],
            device_id={"tile": partner, "rep": rep}, device_id_type=MESH,
        )

    forward(chip, core).start()

    def pass_on(k, carry):
        q, device = group_peer(groups - k)
        spread_copy(device, q).wait_recv()
        forward(q, core).start()
        return carry

    lax.fori_loop(1, groups, pass_on, 0)

    def finish(q, carry):
        forward(q, 1 - core).wait_recv()
        return carry

    lax.fori_loop(0, groups, finish, 0)

    out_ref[...] = gathered[...]

    @pl.when(has_up)
    def _():
        to_up.wait_send()
        grid_up.wait_send()

    @pl.when(has_down)
    def _():
        to_down.wait_send()
        grid_down.wait_send()

    def sent(k, carry):
        peer = tile_peer(k)
        wave_copy(peer, me).wait_send()
        bin_copy(peer, me).wait_send()
        return carry

    lax.fori_loop(1, tiles, sent, 0)
    for a in range(outer):
        swap(a).wait_send()

        @pl.when(at_outer != a)
        def _():
            slab_copy(a, at_outer).wait_send()

    for b in range(inner):

        @pl.when(at_inner != b)
        def _():
            share_copy(b, at_inner).wait_send()


    def shared(k, carry):
        q, device = group_peer(k)
        spread_copy(device, q).wait_send()
        return carry

    lax.fori_loop(1, groups, shared, 0)

    def passed(q, carry):
        forward(q, core).wait_send()
        return carry

    lax.fori_loop(0, groups, passed, 0)


def finish_kernel(
    pred_ref, gathered, pred_out, u1_out, ub_out, u2_out, flat, u1, ub, u2, sem
):
    groups, part, channels = gathered.shape[1:]
    steps = u1.shape[2]
    piece = steps // 2
    small = 9 * piece
    copies = [
        pltpu.make_async_copy(src, dst, sem.at[k])
        for k, (src, dst) in enumerate([(pred_ref, pred_out), (u1, u1_out), (ub, ub_out), (u2, u2_out)])
    ]
    copies[0].start()
    for h in range(2):
        flat[h] = gathered[h].astype(F32).reshape(groups * part, channels)
    one = flat[:, 0:small, :]
    scale = 1.0 / jnp.sqrt(jnp.sum(one * one) / (9 * steps * channels) + 1e-06)
    for k in range(9):
        for h in range(2):
            u1[k // 3, k % 3, h * piece : (h + 1) * piece, :] = flat[h, k * piece : (k + 1) * piece, :] * scale
    copies[1].start()
    two = flat[0, small : small + 24, :] + flat[1, small : small + 24, :]
    two = two / jnp.sqrt(jnp.sum(two * two) / (9 * channels) + 1e-06)
    for i in range(3):
        u2[i] = two[8 * i : 8 * i + 3, :]
    gb = flat[0, small + 24 : small + 25, :] + flat[1, small + 24 : small + 25, :]
    ub[...] = gb / jnp.sqrt(jnp.sum(gb * gb) / channels + 1e-06)
    copies[2].start()
    copies[3].start()
    for copy in copies:
        copy.wait()


def split(tiles, reps):
    half = tiles // 2
    minor = 2 if half % 2 == 0 else 1
    return reps * minor, half // minor


def on_device(tiles, reps, waves, dest_tile, pixel_bin, target, conv_one, bias_one, conv_two, bias_two):
    rows, steps = waves.shape[1:]
    height, width = target.shape[1:]
    channels = conv_one.shape[3]
    pixels = height * width
    groups = tiles // 2 * reps
    small = 9 * (steps // 2)
    part = -(-(small + 32) // (8 * groups)) * 8
    padded = groups * part
    outer, inner = split(tiles, reps)
    hbm = pl.BlockSpec(memory_space=pltpu.HBM)
    tp = -(-(height + 2) // 8) * 8
    dma = pltpu.SemaphoreType.DMA
    vmem = pl.BlockSpec(memory_space=pltpu.VMEM)
    pred, gathered = pl.pallas_call(
        functools.partial(step_kernel, tiles, reps, part),
        out_shape=(
            jax.ShapeDtypeStruct((height, width), F32),
            jax.ShapeDtypeStruct((2, groups, part, channels), BF16),
        ),
        in_specs=[hbm] * 8,
        out_specs=(vmem,) * 2,
        scratch_shapes=[
            pltpu.VMEM((1, rows), jnp.int32),
            pltpu.VMEM((1, rows), jnp.int32),
            pltpu.VMEM((rows, steps), BF16),
            pltpu.VMEM((height, width), F32),
            pltpu.VMEM((3, 3 * steps, channels), BF16),
            pltpu.VMEM((1, channels), F32),
            pltpu.VMEM((3, 3, channels), BF16),
            pltpu.SMEM((1,), F32),
            dma((8,)),
            pltpu.VMEM((tiles * CAP, steps), BF16),
            pltpu.VMEM((tiles, 1, 128), F32),
            pltpu.VMEM((tiles * CAP, steps), BF16),
            pltpu.VMEM((tiles, 1, 128), F32),
            pltpu.VMEM(((height + 2 * HALO) * width, steps), BF16),
            pltpu.VMEM(((height + 2 * HALO) * width, 3 * steps), BF16),
            pltpu.VMEM((pixels, channels), F32),
            pltpu.VMEM(((height + HALO) * width, channels), BF16),
            pltpu.VMEM((height, width), F32),
            pltpu.VMEM((height, width), F32),
            pltpu.VMEM((24, channels), F32),
            pltpu.VMEM((5, tp, width), F32),
            pltpu.VMEM((24, pixels), F32),
            pltpu.VMEM((2, padded, channels), F32),
            pltpu.VMEM((padded, channels), F32),
            pltpu.VMEM((padded, channels), F32),
            pltpu.VMEM((outer, inner * part, channels), F32),
            pltpu.VMEM((inner, part, channels), F32),
            pltpu.VMEM((2, groups, part, channels), BF16),
            dma((tiles,)), dma((tiles,)), dma((tiles,)), dma((tiles,)),
            dma((2,)), dma((2,)), dma((2,)), dma((2,)),
            dma((outer,)), dma((outer,)), dma((outer,)), dma((outer,)), dma((inner,)), dma((inner,)),
            dma((groups,)), dma((groups,)), dma((groups,)), dma((groups,)),
        ],
        compiler_params=pltpu.CompilerParams(
            collective_id=0, has_side_effects=True, vmem_limit_bytes=40 * 1024 * 1024
        ),
        name="step",
    )(
        dest_tile.reshape(1, rows), pixel_bin, waves[0], target[0],
        conv_one.reshape(3, 3 * steps, channels), bias_one.reshape(1, channels), conv_two, bias_two,
    )
    pred, one, bias, two = pl.pallas_call(
        finish_kernel,
        out_shape=(
            jax.ShapeDtypeStruct((height, width), F32),
            jax.ShapeDtypeStruct((3, 3, steps, channels), F32),
            jax.ShapeDtypeStruct((1, channels), F32),
            jax.ShapeDtypeStruct((3, 3, channels), F32),
        ),
        in_specs=[vmem] * 2,
        out_specs=(hbm,) * 4,
        scratch_shapes=[
            pltpu.VMEM((2, padded, channels), F32),
            pltpu.VMEM((3, 3, steps, channels), F32),
            pltpu.VMEM((1, channels), F32),
            pltpu.VMEM((3, 3, channels), F32),
            dma((4,)),
        ],
        name="finish",
    )(pred, gathered)
    return pred[None], one, bias[0], two


def solution(mesh):
    placed = (
        P("rep", "tile", None),
        P("rep", "tile", None),
        P("rep", "tile"),
        P("rep", "tile", None),
        P(),
        P(),
        P(),
        P(),
    )
    return jax.shard_map(
        functools.partial(on_device, mesh.shape["tile"], mesh.shape["rep"]),
        mesh=mesh,
        in_specs=placed,
        out_specs=(P("rep", "tile", None), P(), P(), P()),
        check_vma=False,
    )
```

```python
import functools

import jax
import jax.numpy as jnp
from jax import lax
from jax.experimental import pallas as pl
from jax.experimental.pallas import tpu as pltpu
from jax.sharding import PartitionSpec as P

CAP = 32
HALO = 4
MESH = pl.DeviceIdType.MESH
F32 = jnp.float32
BF16 = jnp.bfloat16


def iota(shape, dim):
    return lax.broadcasted_iota(jnp.int32, shape, dim)


def dot(a, b, dims=((1,), (0,))):
    return lax.dot_general(a, b, (dims, ((), ())), preferred_element_type=F32)


def step_kernel(
    tiles, reps, part,
    dest_hbm, bin_hbm, waves_hbm, target_hbm, w1_hbm, b1_hbm, w2_hbm, b2_hbm,
    pred_ref, out_ref,
    dest_ref, bin_ref, waves_ref, target_ref, w1_ref, b1_ref, w2_ref, b2_ref, l_sem,
    sendw, sendb, recvw, recvb, grid, wide, pre_s, hid_s, tlow, thigh, w2_s, taps, etap,
    full, pair, total, recva, recvs, gathered,
    aw_send, aw_recv, ab_send, ab_recv, t_send, t_recv, g_send, g_recv,
    p_send, p_recv, s_send, s_recv, r_send, r_recv, n_send, n_recv, f_send, f_recv,
):
    me = lax.axis_index("tile")
    rep = lax.axis_index("rep")
    rows, steps = waves_ref.shape
    height, width = target_ref.shape
    channels = b1_ref.shape[1]
    half = tiles // 2
    groups = half * reps
    outer, inner = split(tiles, reps)
    minor = outer // reps
    core = lax.rem(me, 2)
    partner = me + 1 - 2 * core
    at_outer = rep * minor + lax.rem(me // 2, minor)
    at_inner = me // 2 // minor
    chip = at_outer * inner + at_inner
    pixels = height * width
    tall = height + HALO

    def tile_peer(k):
        return lax.rem(me + k, tiles)

    def group_peer(k):
        q = lax.rem(chip + k, groups)
        return q, device_at(q // inner, lax.rem(q, inner))

    def device_at(a, b):
        return {"tile": 2 * (b * minor + lax.rem(a, minor)) + core, "rep": a // minor}

    barrier = pltpu.get_barrier_semaphore()

    def greet(k, carry):
        pl.semaphore_signal(barrier, inc=1, device_id={"tile": tile_peer(k), "rep": rep}, device_id_type=MESH)
        return carry

    lax.fori_loop(1, tiles, greet, 0)

    def greet_far(k, carry):
        pl.semaphore_signal(
            barrier,
            inc=1,
            device_id={"tile": 2 * lax.rem(k, half) + core, "rep": lax.rem(rep + 1 + k // half, reps)},
            device_id_type=MESH,
        )
        return carry

    lax.fori_loop(0, (reps - 1) * half, greet_far, 0)

    loads = [
        pltpu.make_async_copy(src, dst, l_sem.at[k])
        for k, (src, dst) in enumerate(
            [
                (dest_hbm, dest_ref), (bin_hbm, bin_ref), (waves_hbm, waves_ref), (target_hbm, target_ref),
                (w1_hbm, w1_ref), (b1_hbm, b1_ref), (w2_hbm, w2_ref), (b2_hbm, b2_ref),
            ]
        )
    ]
    for load in loads:
        load.start()
    for load in loads[:4]:
        load.wait()

    hits = (iota((tiles, rows), 0) == dest_ref[...]).astype(F32)
    earlier = (iota((rows, rows), 0) < iota((rows, rows), 1)).astype(F32).astype(BF16)
    ranks = dot(hits.astype(BF16), earlier)
    rank = jnp.sum(hits * ranks, axis=0, keepdims=True)
    slot = jnp.sum(hits * (ranks + (CAP * iota((tiles, rows), 0)).astype(F32)), axis=0, keepdims=True)
    place = (iota((tiles * CAP, rows), 0).astype(F32) == slot).astype(F32).astype(BF16)
    sendw[...] = dot(place, waves_ref[...]).astype(BF16)
    lane = rank + (CAP * lax.rem(me, 4)).astype(F32)
    lanes = (iota((128, rows), 0).astype(F32) == lane).astype(F32).astype(BF16)
    bins = bin_ref[...]
    high = (bins // 32).astype(F32)
    low = (bins - 32 * (bins // 32)).astype(F32)
    named = 32.0 * dot((hits * high).astype(BF16), lanes, ((1,), (1,))) + dot(
        (hits * low).astype(BF16), lanes, ((1,), (1,))
    )
    for t in range(tiles):
        sendb[t] = named[t : t + 1, :]

    pl.semaphore_wait(barrier, tiles - 1 + (reps - 1) * half)

    def wave_copy(peer, source):
        return pltpu.make_async_remote_copy(
            src_ref=sendw.at[pl.ds(pl.multiple_of(peer * CAP, CAP), CAP)],
            dst_ref=recvw.at[pl.ds(pl.multiple_of(source * CAP, CAP), CAP)],
            send_sem=aw_send.at[peer],
            recv_sem=aw_recv.at[source],
            device_id={"tile": peer, "rep": rep},
            device_id_type=MESH,
        )

    def bin_copy(peer, source):
        return pltpu.make_async_remote_copy(
            src_ref=sendb.at[peer],
            dst_ref=recvb.at[source],
            send_sem=ab_send.at[peer],
            recv_sem=ab_recv.at[source],
            device_id={"tile": peer, "rep": rep},
            device_id_type=MESH,
        )

    def scatter(k, carry):
        peer = tile_peer(k)
        wave_copy(peer, me).start()
        bin_copy(peer, me).start()
        return carry

    lax.fori_loop(1, tiles, scatter, 0)

    up = jnp.minimum(me + 1, tiles - 1)
    down = jnp.maximum(me - 1, 0)
    span = HALO * width

    def target_copy(peer, dst, k):
        return pltpu.make_async_remote_copy(
            src_ref=target_ref, dst_ref=dst, send_sem=t_send.at[k], recv_sem=t_recv.at[k],
            device_id={"tile": peer, "rep": rep}, device_id_type=MESH,
        )

    def halo_copy(peer, src, dst, k):
        return pltpu.make_async_remote_copy(
            src_ref=grid.at[pl.ds(src, span)], dst_ref=grid.at[pl.ds(dst, span)],
            send_sem=g_send.at[k], recv_sem=g_recv.at[k],
            device_id={"tile": peer, "rep": rep}, device_id_type=MESH,
        )

    to_up = target_copy(up, tlow, 0)
    to_down = target_copy(down, thigh, 1)
    grid_up = halo_copy(up, span + pixels - span, 0, 0)
    grid_down = halo_copy(down, span, span + pixels, 1)
    has_up = me < tiles - 1
    has_down = me > 0

    @pl.when(has_up)
    def _():
        to_up.start()

    @pl.when(has_down)
    def _():
        to_down.start()

    @pl.when(jnp.logical_not(has_down))
    def _():
        grid[0:span, :] = jnp.zeros((span, steps), BF16)
        tlow[...] = jnp.zeros((height, width), F32)

    @pl.when(jnp.logical_not(has_up))
    def _():
        grid[span + pixels : span + pixels + span, :] = jnp.zeros((span, steps), BF16)
        thigh[...] = jnp.zeros((height, width), F32)

    own = pl.ds(pl.multiple_of(me * CAP, CAP), CAP)
    recvw[own, :] = sendw[own, :]
    recvb[me] = sendb[me]
    for load in loads[4:]:
        load.wait()
    w2_s[...] = jnp.zeros(w2_s.shape, F32)
    for i in range(3):
        w2_s[8 * i : 8 * i + 3, :] = w2_ref[i].astype(F32)
    w2 = w2_s[...].astype(BF16)

    def arrive(k, carry):
        peer = tile_peer(k)
        wave_copy(peer, peer).wait_recv()
        bin_copy(peer, peer).wait_recv()
        return carry

    lax.fori_loop(1, tiles, arrive, 0)

    names = []
    for q in range(tiles // 4):
        names.append(recvb[4 * q] + recvb[4 * q + 1] + recvb[4 * q + 2] + recvb[4 * q + 3])
    names = jnp.concatenate(names, axis=1)
    block = 256
    order = [0, pixels - block] + [s for s in range(block, pixels - block, block)]
    for start in order:
        wanted = (iota((block, tiles * CAP), 0) + start).astype(F32)
        onehot = (wanted == names).astype(F32).astype(BF16)
        grid[span + start : span + start + block, :] = dot(onehot, recvw[...]).astype(BF16)

    @pl.when(has_up)
    def _():
        grid_up.start()

    @pl.when(has_down)
    def _():
        grid_down.start()

    column = iota((width, steps), 0)

    def spread(y):
        line = grid[y * width : (y + 1) * width, :]
        value = line.astype(F32)
        left = jnp.where(column >= 2, pltpu.roll(value, 2, 0), 0.0)
        right = jnp.where(column < width - 2, pltpu.roll(value, width - 2, 0), 0.0)
        wide[y * width : (y + 1) * width, 0:steps] = left.astype(BF16)
        wide[y * width : (y + 1) * width, steps : 2 * steps] = line
        wide[y * width : (y + 1) * width, 2 * steps : 3 * steps] = right.astype(BF16)

    for y in range(HALO, HALO + height):
        spread(y)

    bias = b1_ref[...]

    def convolve(y):
        acc = jnp.zeros((2 * width, channels), F32) + bias
        for i in range(3):
            acc = acc + dot(wide[(y + 2 * i) * width : (y + 2 * i + 2) * width, :], w1_ref[i])
        sig = 1.0 / (1.0 + jnp.exp(-acc))
        hidden = acc * sig
        if y < 2:
            hidden = jnp.where(has_down, hidden, 0.0)
        if y >= height + 2:
            hidden = jnp.where(has_up, hidden, 0.0)
        hid_s[y * width : (y + 2) * width, :] = hidden.astype(BF16)
        if 2 <= y < height + 2:
            pre_s[(y - 2) * width : y * width, :] = sig * (1.0 + acc * (1.0 - sig))

    middle = [y for y in range(HALO, height, 2)]
    for y in middle:
        convolve(y)

    @pl.when(has_down)
    def _():
        grid_up.wait_recv()

    @pl.when(has_up)
    def _():
        grid_down.wait_recv()

    for y in list(range(HALO)) + list(range(HALO + height, 2 * HALO + height)):
        spread(y)

    for y in range(0, tall, 2):
        if y not in middle:
            convolve(y)

    each = dot(w2, hid_s[...], ((1,), (1,)))
    span2 = (height + 2) * width
    summed = each[0:8, 0:span2] + each[8:16, width : width + span2] + each[16:24, 2 * width : 2 * width + span2]
    taps[...] = jnp.zeros(taps.shape, F32)
    for y in range(height + 2):
        for j in range(3):
            taps[j, y : y + 1, :] = summed[j : j + 1, y * width : (y + 1) * width]
    tp = taps.shape[1]
    x_at = iota((tp, width), 1)
    y_at = iota((tp, width), 0)
    pred = (
        b2_ref[0]
        + jnp.where(x_at >= 1, pltpu.roll(taps[0], 1, 1), 0.0)
        + taps[1]
        + jnp.where(x_at < width - 1, pltpu.roll(taps[2], width - 1, 1), 0.0)
    )

    @pl.when(has_down)
    def _():
        to_up.wait_recv()

    @pl.when(has_up)
    def _():
        to_down.wait_recv()

    taps[3] = pred
    pred_ref[...] = taps[3, 1 : 1 + height, :]
    taps[4, 0:1, :] = tlow[height - 1 : height, :]
    taps[4, 1 : 1 + height, :] = target_ref[...]
    taps[4, 1 + height : 2 + height, :] = thigh[0:1, :]
    inside = jnp.logical_and(
        jnp.logical_or(y_at >= 1, has_down),
        jnp.logical_and(y_at < height + 2, jnp.logical_or(y_at < height + 1, has_up)),
    )
    error = jnp.where(inside, (pred - taps[4]) / reps, 0.0).astype(BF16).astype(F32)
    taps[0] = jnp.where(x_at < width - 1, pltpu.roll(error, width - 1, 1), 0.0)
    taps[1] = error
    taps[2] = jnp.where(x_at >= 1, pltpu.roll(error, 1, 1), 0.0)
    etap[...] = jnp.zeros(etap.shape, F32)
    for i in range(3):
        for j in range(3):
            for y in range(height):
                etap[8 * i + j : 8 * i + j + 1, y * width : (y + 1) * width] = taps[j, y + 2 - i : y + 3 - i, :]
    errors = etap[...].astype(BF16)

    mine = hid_s[2 * width : 2 * width + pixels, :]
    grad_two = dot(errors, mine)
    back = dot(errors, w2, ((0,), (0,)))
    slope = (back * pre_s[...]).astype(BF16)
    grad_bias = dot(jnp.ones((8, pixels), BF16), slope)
    piece = steps // 2
    small = 9 * piece
    for h in range(2):
        full[h, small : small + 24, :] = grad_two
        full[h, small + 24 : small + 32, :] = grad_bias
        if full.shape[1] > small + 32:
            full[h, small + 32 :, :] = jnp.zeros((full.shape[1] - small - 32, channels), F32)
    slab = inner * part

    def swap(a):
        rows_a = pl.ds(a * slab, slab)
        return pltpu.make_async_remote_copy(
            src_ref=full.at[1 - core, rows_a], dst_ref=pair.at[rows_a],
            send_sem=p_send.at[a], recv_sem=p_recv.at[a],
            device_id={"tile": partner, "rep": rep}, device_id_type=MESH,
        )

    started = 0
    for i in range(3):
        start = (2 + 2 * i) * width
        g = dot(wide[start : start + pixels, :], slope, ((0,), (0,)))
        for j in range(3):
            k = 3 * i + j
            for h in range(2):
                full[h, k * piece : (k + 1) * piece, :] = g[j * steps + h * piece : j * steps + (h + 1) * piece, :]
        while started < outer and ((started + 1) * slab <= 3 * (i + 1) * piece or i == 2):
            swap(started).start()
            started += 1

    def slab_copy(a, source):
        return pltpu.make_async_remote_copy(
            src_ref=total.at[pl.ds(a * slab, slab)], dst_ref=recva.at[source],
            send_sem=s_send.at[a], recv_sem=s_recv.at[source],
            device_id=device_at(a, at_inner), device_id_type=MESH,
        )

    for a in range(outer):
        swap(a).wait_recv()
        rows_a = slice(a * slab, (a + 1) * slab)
        total[rows_a, :] = full[core, rows_a, :] + pair[rows_a, :]

        @pl.when(at_outer != a)
        def _():
            slab_copy(a, at_outer).start()

    recva[at_outer] = total[pl.ds(pl.multiple_of(at_outer * slab, 8), slab), :]
    for a in range(outer):

        @pl.when(at_outer != a)
        def _():
            slab_copy(a, a).wait_recv()

    plane = recva[0]
    for a in range(1, outer):
        plane = plane + recva[a]
    pair[0:slab, :] = plane

    def share_copy(b, source):
        return pltpu.make_async_remote_copy(
            src_ref=pair.at[pl.ds(b * part, part)], dst_ref=recvs.at[source],
            send_sem=r_send.at[b], recv_sem=r_recv.at[source],
            device_id=device_at(at_outer, b), device_id_type=MESH,
        )

    for b in range(inner):

        @pl.when(at_inner != b)
        def _():
            share_copy(b, at_inner).start()

    recvs[at_inner] = pair[pl.ds(pl.multiple_of(at_inner * part, 8), part), :]
    for b in range(inner):

        @pl.when(at_inner != b)
        def _():
            share_copy(b, b).wait_recv()

    share = recvs[0]
    for b in range(1, inner):
        share = share + recvs[b]
    rest = share - share.astype(BF16).astype(F32)
    tail = jnp.logical_and(iota(share.shape, 0) + chip * part >= small, core == 1)
    gathered[core, chip] = jnp.where(tail, rest, share).astype(BF16)

    def spread_copy(device, source):
        return pltpu.make_async_remote_copy(
            src_ref=gathered.at[core, chip], dst_ref=gathered.at[core, source],
            send_sem=n_send.at[source], recv_sem=n_recv.at[source], device_id=device, device_id_type=MESH,
        )

    def spread_start(k, carry):
        q, device = group_peer(k)
        pltpu.make_async_remote_copy(
            src_ref=gathered.at[core, chip], dst_ref=gathered.at[core, chip],
            send_sem=n_send.at[q], recv_sem=n_recv.at[chip], device_id=device, device_id_type=MESH,
        ).start()
        return carry

    lax.fori_loop(1, groups, spread_start, 0)

    def forward(q, which):
        return pltpu.make_async_remote_copy(
            src_ref=gathered.at[which, q], dst_ref=gathered.at[which, q],
            send_sem=f_send.at[q], recv_sem=f_recv.at[q],
            device_id={"tile": partner, "rep": rep}, device_id_type=MESH,
        )

    forward(chip, core).start()

    def pass_on(k, carry):
        q, device = group_peer(groups - k)
        spread_copy(device, q).wait_recv()
        forward(q, core).start()
        return carry

    lax.fori_loop(1, groups, pass_on, 0)

    def finish(q, carry):
        forward(q, 1 - core).wait_recv()
        return carry

    lax.fori_loop(0, groups, finish, 0)

    out_ref[...] = gathered[...]

    @pl.when(has_up)
    def _():
        to_up.wait_send()
        grid_up.wait_send()

    @pl.when(has_down)
    def _():
        to_down.wait_send()
        grid_down.wait_send()

    def sent(k, carry):
        peer = tile_peer(k)
        wave_copy(peer, me).wait_send()
        bin_copy(peer, me).wait_send()
        return carry

    lax.fori_loop(1, tiles, sent, 0)
    for a in range(outer):
        swap(a).wait_send()

        @pl.when(at_outer != a)
        def _():
            slab_copy(a, at_outer).wait_send()

    for b in range(inner):

        @pl.when(at_inner != b)
        def _():
            share_copy(b, at_inner).wait_send()


    def shared(k, carry):
        q, device = group_peer(k)
        spread_copy(device, q).wait_send()
        return carry

    lax.fori_loop(1, groups, shared, 0)

    def passed(q, carry):
        forward(q, core).wait_send()
        return carry

    lax.fori_loop(0, groups, passed, 0)


def finish_kernel(
    pred_ref, gathered, pred_out, u1_out, ub_out, u2_out, flat, u1, ub, u2, sem
):
    groups, part, channels = gathered.shape[1:]
    steps = u1.shape[2]
    piece = steps // 2
    small = 9 * piece
    copies = [
        pltpu.make_async_copy(src, dst, sem.at[k])
        for k, (src, dst) in enumerate([(pred_ref, pred_out), (u1, u1_out), (ub, ub_out), (u2, u2_out)])
    ]
    copies[0].start()
    for h in range(2):
        flat[h] = gathered[h].astype(F32).reshape(groups * part, channels)
    one = flat[:, 0:small, :]
    scale = 1.0 / jnp.sqrt(jnp.sum(one * one) / (9 * steps * channels) + 1e-06)
    for k in range(9):
        for h in range(2):
            u1[k // 3, k % 3, h * piece : (h + 1) * piece, :] = flat[h, k * piece : (k + 1) * piece, :] * scale
    copies[1].start()
    two = flat[0, small : small + 24, :] + flat[1, small : small + 24, :]
    two = two / jnp.sqrt(jnp.sum(two * two) / (9 * channels) + 1e-06)
    for i in range(3):
        u2[i] = two[8 * i : 8 * i + 3, :]
    gb = flat[0, small + 24 : small + 25, :] + flat[1, small + 24 : small + 25, :]
    ub[...] = gb / jnp.sqrt(jnp.sum(gb * gb) / channels + 1e-06)
    copies[2].start()
    copies[3].start()
    for copy in copies:
        copy.wait()


def split(tiles, reps):
    half = tiles // 2
    minor = 2 if half % 2 == 0 else 1
    return reps * minor, half // minor


def on_device(tiles, reps, waves, dest_tile, pixel_bin, target, conv_one, bias_one, conv_two, bias_two):
    rows, steps = waves.shape[1:]
    height, width = target.shape[1:]
    channels = conv_one.shape[3]
    pixels = height * width
    groups = tiles // 2 * reps
    small = 9 * (steps // 2)
    part = -(-(small + 32) // (8 * groups)) * 8
    padded = groups * part
    outer, inner = split(tiles, reps)
    hbm = pl.BlockSpec(memory_space=pltpu.HBM)
    tp = -(-(height + 2) // 8) * 8
    dma = pltpu.SemaphoreType.DMA
    vmem = pl.BlockSpec(memory_space=pltpu.VMEM)
    pred, gathered = pl.pallas_call(
        functools.partial(step_kernel, tiles, reps, part),
        out_shape=(
            jax.ShapeDtypeStruct((height, width), F32),
            jax.ShapeDtypeStruct((2, groups, part, channels), BF16),
        ),
        in_specs=[hbm] * 8,
        out_specs=(vmem,) * 2,
        scratch_shapes=[
            pltpu.VMEM((1, rows), jnp.int32),
            pltpu.VMEM((1, rows), jnp.int32),
            pltpu.VMEM((rows, steps), BF16),
            pltpu.VMEM((height, width), F32),
            pltpu.VMEM((3, 3 * steps, channels), BF16),
            pltpu.VMEM((1, channels), F32),
            pltpu.VMEM((3, 3, channels), BF16),
            pltpu.SMEM((1,), F32),
            dma((8,)),
            pltpu.VMEM((tiles * CAP, steps), BF16),
            pltpu.VMEM((tiles, 1, 128), F32),
            pltpu.VMEM((tiles * CAP, steps), BF16),
            pltpu.VMEM((tiles, 1, 128), F32),
            pltpu.VMEM(((height + 2 * HALO) * width, steps), BF16),
            pltpu.VMEM(((height + 2 * HALO) * width, 3 * steps), BF16),
            pltpu.VMEM((pixels, channels), F32),
            pltpu.VMEM(((height + HALO) * width, channels), BF16),
            pltpu.VMEM((height, width), F32),
            pltpu.VMEM((height, width), F32),
            pltpu.VMEM((24, channels), F32),
            pltpu.VMEM((5, tp, width), F32),
            pltpu.VMEM((24, pixels), F32),
            pltpu.VMEM((2, padded, channels), F32),
            pltpu.VMEM((padded, channels), F32),
            pltpu.VMEM((padded, channels), F32),
            pltpu.VMEM((outer, inner * part, channels), F32),
            pltpu.VMEM((inner, part, channels), F32),
            pltpu.VMEM((2, groups, part, channels), BF16),
            dma((tiles,)), dma((tiles,)), dma((tiles,)), dma((tiles,)),
            dma((2,)), dma((2,)), dma((2,)), dma((2,)),
            dma((outer,)), dma((outer,)), dma((outer,)), dma((outer,)), dma((inner,)), dma((inner,)),
            dma((groups,)), dma((groups,)), dma((groups,)), dma((groups,)),
        ],
        compiler_params=pltpu.CompilerParams(
            collective_id=0, has_side_effects=True, vmem_limit_bytes=60 * 1024 * 1024
        ),
        name="step",
    )(
        dest_tile.reshape(1, rows), pixel_bin, waves[0], target[0],
        conv_one.reshape(3, 3 * steps, channels), bias_one.reshape(1, channels), conv_two, bias_two,
    )
    pred, one, bias, two = pl.pallas_call(
        finish_kernel,
        out_shape=(
            jax.ShapeDtypeStruct((height, width), F32),
            jax.ShapeDtypeStruct((3, 3, steps, channels), F32),
            jax.ShapeDtypeStruct((1, channels), F32),
            jax.ShapeDtypeStruct((3, 3, channels), F32),
        ),
        in_specs=[vmem] * 2,
        out_specs=(hbm,) * 4,
        scratch_shapes=[
            pltpu.VMEM((2, padded, channels), F32),
            pltpu.VMEM((3, 3, steps, channels), F32),
            pltpu.VMEM((1, channels), F32),
            pltpu.VMEM((3, 3, channels), F32),
            dma((4,)),
        ],
        name="finish",
    )(pred, gathered)
    return pred[None], one, bias[0], two


def solution(mesh):
    placed = (
        P("rep", "tile", None),
        P("rep", "tile", None),
        P("rep", "tile"),
        P("rep", "tile", None),
        P(),
        P(),
        P(),
        P(),
    )
    return jax.shard_map(
        functools.partial(on_device, mesh.shape["tile"], mesh.shape["rep"]),
        mesh=mesh,
        in_specs=placed,
        out_specs=(P("rep", "tile", None), P(), P(), P()),
        check_vma=False,
    )
```

```python
import functools

import jax
import jax.numpy as jnp
from jax import lax
from jax.experimental import pallas as pl
from jax.experimental.pallas import tpu as pltpu
from jax.sharding import PartitionSpec as P

CAP = 32
HALO = 4
MESH = pl.DeviceIdType.MESH
F32 = jnp.float32
BF16 = jnp.bfloat16


def iota(shape, dim):
    return lax.broadcasted_iota(jnp.int32, shape, dim)


def dot(a, b, dims=((1,), (0,))):
    return lax.dot_general(a, b, (dims, ((), ())), preferred_element_type=F32)


def step_kernel(
    tiles, reps, part,
    dest_hbm, bin_hbm, waves_hbm, target_hbm, w1_hbm, b1_hbm, w2_hbm, b2_hbm,
    pred_ref, out_ref,
    dest_ref, bin_ref, waves_ref, target_ref, w1_ref, b1_ref, w2_ref, b2_ref, l_sem,
    sendw, recvw, grid, wide, pre_s, hid_s, tlow, thigh, w2_s, taps, etap,
    full, pair, total, recva, recvs, gathered,
    aw_send, aw_recv, t_send, t_recv, g_send, g_recv,
    p_send, p_recv, s_send, s_recv, r_send, r_recv, n_send, n_recv, m_send, m_recv, f_send, f_recv,
):
    me = lax.axis_index("tile")
    rep = lax.axis_index("rep")
    rows, steps = waves_ref.shape
    height, width = target_ref.shape
    channels = b1_ref.shape[1]
    half = tiles // 2
    groups = half * reps
    outer, inner = split(tiles, reps)
    minor = outer // reps
    core = lax.rem(me, 2)
    partner = me + 1 - 2 * core
    at_outer = rep * minor + lax.rem(me // 2, minor)
    at_inner = me // 2 // minor
    chip = at_outer * inner + at_inner
    pixels = height * width
    tall = height + HALO

    def tile_peer(k):
        return lax.rem(me + k, tiles)

    def device_at(a, b):
        return {"tile": 2 * (b * minor + lax.rem(a, minor)) + core, "rep": a // minor}

    barrier = pltpu.get_barrier_semaphore()

    def greet(k, carry):
        pl.semaphore_signal(barrier, inc=1, device_id={"tile": tile_peer(k), "rep": rep}, device_id_type=MESH)
        return carry

    lax.fori_loop(1, tiles, greet, 0)

    def greet_far(k, carry):
        pl.semaphore_signal(
            barrier,
            inc=1,
            device_id={
                "tile": 2 * (at_inner * minor + lax.rem(k, minor)) + core,
                "rep": lax.rem(rep + 1 + k // minor, reps),
            },
            device_id_type=MESH,
        )
        return carry

    lax.fori_loop(0, (reps - 1) * minor, greet_far, 0)
    loads = [
        pltpu.make_async_copy(src, dst, l_sem.at[k])
        for k, (src, dst) in enumerate(
            [
                (dest_hbm, dest_ref), (bin_hbm, bin_ref), (waves_hbm, waves_ref), (target_hbm, target_ref),
                (w1_hbm, w1_ref), (b1_hbm, b1_ref), (w2_hbm, w2_ref), (b2_hbm, b2_ref),
            ]
        )
    ]
    for load in loads:
        load.start()
    for load in loads[:4]:
        load.wait()

    hits = (iota((tiles, rows), 0) == dest_ref[...]).astype(F32)
    earlier = (iota((rows, rows), 0) < iota((rows, rows), 1)).astype(F32).astype(BF16)
    ranks = dot(hits.astype(BF16), earlier)
    rank = jnp.sum(hits * ranks, axis=0, keepdims=True)
    slot = jnp.sum(hits * (ranks + (CAP * iota((tiles, rows), 0)).astype(F32)), axis=0, keepdims=True)
    place = (iota((tiles * CAP, rows), 0).astype(F32) == slot).astype(F32).astype(BF16)
    sendw[:, 0:CAP, :] = dot(place, waves_ref[...]).astype(BF16).reshape(tiles, CAP, steps)
    lane = rank + (CAP * lax.rem(me, 4)).astype(F32)
    lanes = (iota((128, rows), 0).astype(F32) == lane).astype(F32).astype(BF16)
    bins = bin_ref[...]
    high = (bins // 32).astype(F32)
    low = (bins - 32 * (bins // 32)).astype(F32)
    highs = dot((hits * high).astype(BF16), lanes, ((1,), (1,)))
    lows = dot((hits * low).astype(BF16), lanes, ((1,), (1,)))
    turn = iota((8, 128), 0)
    for t in range(tiles):
        both = jnp.where(turn == 0, highs[t : t + 1, :], jnp.where(turn == 1, lows[t : t + 1, :], 0.0))
        sendw[t, CAP:, :] = both.astype(BF16)

    pl.semaphore_wait(barrier, tiles - 1 + (reps - 1) * minor)

    def wave_copy(peer, source):
        return pltpu.make_async_remote_copy(
            src_ref=sendw.at[peer],
            dst_ref=recvw.at[source],
            send_sem=aw_send.at[peer],
            recv_sem=aw_recv.at[source],
            device_id={"tile": peer, "rep": rep},
            device_id_type=MESH,
        )

    def scatter(k, carry):
        peer = tile_peer(k)
        wave_copy(peer, me).start()
        return carry

    lax.fori_loop(1, tiles, scatter, 0)

    up = jnp.minimum(me + 1, tiles - 1)
    down = jnp.maximum(me - 1, 0)
    span = HALO * width

    def target_copy(peer, dst, k):
        return pltpu.make_async_remote_copy(
            src_ref=target_ref, dst_ref=dst, send_sem=t_send.at[k], recv_sem=t_recv.at[k],
            device_id={"tile": peer, "rep": rep}, device_id_type=MESH,
        )

    def halo_copy(peer, src, dst, k):
        return pltpu.make_async_remote_copy(
            src_ref=grid.at[pl.ds(src, span)], dst_ref=grid.at[pl.ds(dst, span)],
            send_sem=g_send.at[k], recv_sem=g_recv.at[k],
            device_id={"tile": peer, "rep": rep}, device_id_type=MESH,
        )

    to_up = target_copy(up, tlow, 0)
    to_down = target_copy(down, thigh, 1)
    grid_up = halo_copy(up, span + pixels - span, 0, 0)
    grid_down = halo_copy(down, span, span + pixels, 1)
    has_up = me < tiles - 1
    has_down = me > 0

    @pl.when(has_up)
    def _():
        to_up.start()

    @pl.when(has_down)
    def _():
        to_down.start()

    @pl.when(jnp.logical_not(has_down))
    def _():
        grid[0:span, :] = jnp.zeros((span, steps), BF16)
        tlow[...] = jnp.zeros((height, width), F32)

    @pl.when(jnp.logical_not(has_up))
    def _():
        grid[span + pixels : span + pixels + span, :] = jnp.zeros((span, steps), BF16)
        thigh[...] = jnp.zeros((height, width), F32)

    recvw[me] = sendw[me]
    for load in loads[4:]:
        load.wait()
    w2_s[...] = jnp.zeros(w2_s.shape, F32)
    for i in range(3):
        w2_s[8 * i : 8 * i + 3, :] = w2_ref[i].astype(F32)
    w2 = w2_s[...].astype(BF16)

    def arrive(k, carry):
        peer = tile_peer(k)
        wave_copy(peer, peer).wait_recv()
        return carry

    lax.fori_loop(1, tiles, arrive, 0)

    names = []
    for q in range(tiles // 4):
        both = recvw[4 * q, CAP:, :].astype(F32)
        for t in range(4 * q + 1, 4 * q + 4):
            both = both + recvw[t, CAP:, :].astype(F32)
        names.append(32.0 * both[0:1, :] + both[1:2, :])
    names = jnp.concatenate(names, axis=1)
    block = 256
    arrived = recvw[:, 0:CAP, :].reshape(tiles * CAP, steps)
    order = [0, pixels - block] + [s for s in range(block, pixels - block, block)]
    for start in order:
        wanted = (iota((block, tiles * CAP), 0) + start).astype(F32)
        onehot = (wanted == names).astype(F32).astype(BF16)
        grid[span + start : span + start + block, :] = dot(onehot, arrived).astype(BF16)

    @pl.when(has_up)
    def _():
        grid_up.start()

    @pl.when(has_down)
    def _():
        grid_down.start()

    column = iota((width, steps), 0)

    def spread(y):
        line = grid[y * width : (y + 1) * width, :]
        value = line.astype(F32)
        left = jnp.where(column >= 2, pltpu.roll(value, 2, 0), 0.0)
        right = jnp.where(column < width - 2, pltpu.roll(value, width - 2, 0), 0.0)
        wide[y * width : (y + 1) * width, 0:steps] = left.astype(BF16)
        wide[y * width : (y + 1) * width, steps : 2 * steps] = line
        wide[y * width : (y + 1) * width, 2 * steps : 3 * steps] = right.astype(BF16)

    for y in range(HALO, HALO + height):
        spread(y)

    bias = b1_ref[...]

    def convolve(y):
        acc = jnp.zeros((2 * width, channels), F32) + bias
        for i in range(3):
            acc = acc + dot(wide[(y + 2 * i) * width : (y + 2 * i + 2) * width, :], w1_ref[i])
        sig = 1.0 / (1.0 + jnp.exp(-acc))
        hidden = acc * sig
        if y < 2:
            hidden = jnp.where(has_down, hidden, 0.0)
        if y >= height + 2:
            hidden = jnp.where(has_up, hidden, 0.0)
        hid_s[y * width : (y + 2) * width, :] = hidden.astype(BF16)
        if 2 <= y < height + 2:
            pre_s[(y - 2) * width : y * width, :] = sig * (1.0 + acc * (1.0 - sig))

    middle = [y for y in range(HALO, height, 2)]
    for y in middle:
        convolve(y)

    @pl.when(has_down)
    def _():
        grid_up.wait_recv()

    @pl.when(has_up)
    def _():
        grid_down.wait_recv()

    for y in list(range(HALO)) + list(range(HALO + height, 2 * HALO + height)):
        spread(y)

    for y in range(0, tall, 2):
        if y not in middle:
            convolve(y)

    each = dot(w2, hid_s[...], ((1,), (1,)))
    span2 = (height + 2) * width
    summed = each[0:8, 0:span2] + each[8:16, width : width + span2] + each[16:24, 2 * width : 2 * width + span2]
    taps[...] = jnp.zeros(taps.shape, F32)
    for y in range(height + 2):
        for j in range(3):
            taps[j, y : y + 1, :] = summed[j : j + 1, y * width : (y + 1) * width]
    tp = taps.shape[1]
    x_at = iota((tp, width), 1)
    y_at = iota((tp, width), 0)
    pred = (
        b2_ref[0]
        + jnp.where(x_at >= 1, pltpu.roll(taps[0], 1, 1), 0.0)
        + taps[1]
        + jnp.where(x_at < width - 1, pltpu.roll(taps[2], width - 1, 1), 0.0)
    )

    @pl.when(has_down)
    def _():
        to_up.wait_recv()

    @pl.when(has_up)
    def _():
        to_down.wait_recv()

    taps[3] = pred
    pred_ref[...] = taps[3, 1 : 1 + height, :]
    taps[4, 0:1, :] = tlow[height - 1 : height, :]
    taps[4, 1 : 1 + height, :] = target_ref[...]
    taps[4, 1 + height : 2 + height, :] = thigh[0:1, :]
    inside = jnp.logical_and(
        jnp.logical_or(y_at >= 1, has_down),
        jnp.logical_and(y_at < height + 2, jnp.logical_or(y_at < height + 1, has_up)),
    )
    error = jnp.where(inside, (pred - taps[4]) / reps, 0.0).astype(BF16).astype(F32)
    taps[0] = jnp.where(x_at < width - 1, pltpu.roll(error, width - 1, 1), 0.0)
    taps[1] = error
    taps[2] = jnp.where(x_at >= 1, pltpu.roll(error, 1, 1), 0.0)
    etap[...] = jnp.zeros(etap.shape, F32)
    for i in range(3):
        for j in range(3):
            for y in range(height):
                etap[8 * i + j : 8 * i + j + 1, y * width : (y + 1) * width] = taps[j, y + 2 - i : y + 3 - i, :]
    errors = etap[...].astype(BF16)

    mine = hid_s[2 * width : 2 * width + pixels, :]
    grad_two = dot(errors, mine)
    back = dot(errors, w2, ((0,), (0,)))
    slope = (back * pre_s[...]).astype(BF16)
    grad_bias = dot(jnp.ones((8, pixels), BF16), slope)
    piece = steps // 2
    small = 9 * piece
    for h in range(2):
        full[h, small : small + 24, :] = grad_two
        full[h, small + 24 : small + 32, :] = grad_bias
        if full.shape[1] > small + 32:
            full[h, small + 32 :, :] = jnp.zeros((full.shape[1] - small - 32, channels), F32)
    slab = inner * part

    def swap(a):
        rows_a = pl.ds(a * slab, slab)
        return pltpu.make_async_remote_copy(
            src_ref=full.at[1 - core, rows_a], dst_ref=pair.at[rows_a],
            send_sem=p_send.at[a], recv_sem=p_recv.at[a],
            device_id={"tile": partner, "rep": rep}, device_id_type=MESH,
        )

    started = 0
    for i in range(3):
        start = (2 + 2 * i) * width
        g = dot(wide[start : start + pixels, :], slope, ((0,), (0,)))
        for j in range(3):
            k = 3 * i + j
            for h in range(2):
                full[h, k * piece : (k + 1) * piece, :] = g[j * steps + h * piece : j * steps + (h + 1) * piece, :]
        while started < outer and ((started + 1) * slab <= 3 * (i + 1) * piece or i == 2):
            swap(started).start()
            started += 1

    def slab_copy(a, source):
        return pltpu.make_async_remote_copy(
            src_ref=total.at[pl.ds(a * slab, slab)], dst_ref=recva.at[source],
            send_sem=s_send.at[a], recv_sem=s_recv.at[source],
            device_id=device_at(a, at_inner), device_id_type=MESH,
        )

    for a in range(outer):
        swap(a).wait_recv()
        rows_a = slice(a * slab, (a + 1) * slab)
        total[rows_a, :] = full[core, rows_a, :] + pair[rows_a, :]

        @pl.when(at_outer != a)
        def _():
            slab_copy(a, at_outer).start()

    recva[at_outer] = total[pl.ds(pl.multiple_of(at_outer * slab, 8), slab), :]
    for a in range(outer):

        @pl.when(at_outer != a)
        def _():
            slab_copy(a, a).wait_recv()

    plane = recva[0]
    for a in range(1, outer):
        plane = plane + recva[a]
    pair[0:slab, :] = plane

    def share_copy(b, source):
        return pltpu.make_async_remote_copy(
            src_ref=pair.at[pl.ds(b * part, part)], dst_ref=recvs.at[source],
            send_sem=r_send.at[b], recv_sem=r_recv.at[source],
            device_id=device_at(at_outer, b), device_id_type=MESH,
        )

    for b in range(inner):

        @pl.when(at_inner != b)
        def _():
            share_copy(b, at_inner).start()

    recvs[at_inner] = pair[pl.ds(pl.multiple_of(at_inner * part, 8), part), :]
    for b in range(inner):

        @pl.when(at_inner != b)
        def _():
            share_copy(b, b).wait_recv()

    share = recvs[0]
    for b in range(1, inner):
        share = share + recvs[b]
    rest = share - share.astype(BF16).astype(F32)
    tail = jnp.logical_and(iota(share.shape, 0) + chip * part >= small, core == 1)
    gathered[core, chip] = jnp.where(tail, rest, share).astype(BF16)

    def line_copy(b, source):
        spot = at_outer * inner + source
        return pltpu.make_async_remote_copy(
            src_ref=gathered.at[core, spot], dst_ref=gathered.at[core, spot],
            send_sem=n_send.at[b], recv_sem=n_recv.at[source],
            device_id=device_at(at_outer, b), device_id_type=MESH,
        )

    def plane_copy(a, source):
        spots = pl.ds(source * inner, inner)
        return pltpu.make_async_remote_copy(
            src_ref=gathered.at[core, spots], dst_ref=gathered.at[core, spots],
            send_sem=m_send.at[a], recv_sem=m_recv.at[source],
            device_id=device_at(a, at_inner), device_id_type=MESH,
        )

    def forward(a, which):
        spots = pl.ds(a * inner, inner)
        return pltpu.make_async_remote_copy(
            src_ref=gathered.at[which, spots], dst_ref=gathered.at[which, spots],
            send_sem=f_send.at[a], recv_sem=f_recv.at[a],
            device_id={"tile": partner, "rep": rep}, device_id_type=MESH,
        )

    for b in range(inner):

        @pl.when(at_inner != b)
        def _():
            line_copy(b, at_inner).start()

    for b in range(inner):

        @pl.when(at_inner != b)
        def _():
            line_copy(b, b).wait_recv()

    for a in range(outer):

        @pl.when(at_outer != a)
        def _():
            plane_copy(a, at_outer).start()

    forward(at_outer, core).start()
    for a in range(outer):

        @pl.when(at_outer != a)
        def _():
            plane_copy(a, a).wait_recv()
            forward(a, core).start()

    for a in range(outer):
        forward(a, 1 - core).wait_recv()

    out_ref[...] = gathered[...]

    @pl.when(has_up)
    def _():
        to_up.wait_send()
        grid_up.wait_send()

    @pl.when(has_down)
    def _():
        to_down.wait_send()
        grid_down.wait_send()

    def sent(k, carry):
        peer = tile_peer(k)
        wave_copy(peer, me).wait_send()
        return carry

    lax.fori_loop(1, tiles, sent, 0)
    for a in range(outer):
        swap(a).wait_send()

        @pl.when(at_outer != a)
        def _():
            slab_copy(a, at_outer).wait_send()

    for b in range(inner):

        @pl.when(at_inner != b)
        def _():
            share_copy(b, at_inner).wait_send()


    for b in range(inner):

        @pl.when(at_inner != b)
        def _():
            line_copy(b, at_inner).wait_send()

    for a in range(outer):
        forward(a, core).wait_send()

        @pl.when(at_outer != a)
        def _():
            plane_copy(a, at_outer).wait_send()


def finish_kernel(
    pred_ref, gathered, pred_out, u1_out, ub_out, u2_out, flat, u1, ub, u2, sem
):
    groups, part, channels = gathered.shape[1:]
    steps = u1.shape[2]
    piece = steps // 2
    small = 9 * piece
    copies = [
        pltpu.make_async_copy(src, dst, sem.at[k])
        for k, (src, dst) in enumerate([(pred_ref, pred_out), (u1, u1_out), (ub, ub_out), (u2, u2_out)])
    ]
    copies[0].start()
    for h in range(2):
        flat[h] = gathered[h].astype(F32).reshape(groups * part, channels)
    one = flat[:, 0:small, :]
    scale = 1.0 / jnp.sqrt(jnp.sum(one * one) / (9 * steps * channels) + 1e-06)
    for k in range(9):
        for h in range(2):
            u1[k // 3, k % 3, h * piece : (h + 1) * piece, :] = flat[h, k * piece : (k + 1) * piece, :] * scale
    copies[1].start()
    two = flat[0, small : small + 24, :] + flat[1, small : small + 24, :]
    two = two / jnp.sqrt(jnp.sum(two * two) / (9 * channels) + 1e-06)
    for i in range(3):
        u2[i] = two[8 * i : 8 * i + 3, :]
    gb = flat[0, small + 24 : small + 25, :] + flat[1, small + 24 : small + 25, :]
    ub[...] = gb / jnp.sqrt(jnp.sum(gb * gb) / channels + 1e-06)
    copies[2].start()
    copies[3].start()
    for copy in copies:
        copy.wait()


def split(tiles, reps):
    half = tiles // 2
    minor = 2 if half % 2 == 0 else 1
    return reps * minor, half // minor


def on_device(tiles, reps, waves, dest_tile, pixel_bin, target, conv_one, bias_one, conv_two, bias_two):
    rows, steps = waves.shape[1:]
    height, width = target.shape[1:]
    channels = conv_one.shape[3]
    pixels = height * width
    groups = tiles // 2 * reps
    small = 9 * (steps // 2)
    part = -(-(small + 32) // (8 * groups)) * 8
    padded = groups * part
    outer, inner = split(tiles, reps)
    hbm = pl.BlockSpec(memory_space=pltpu.HBM)
    tp = -(-(height + 2) // 8) * 8
    dma = pltpu.SemaphoreType.DMA
    vmem = pl.BlockSpec(memory_space=pltpu.VMEM)
    pred, gathered = pl.pallas_call(
        functools.partial(step_kernel, tiles, reps, part),
        out_shape=(
            jax.ShapeDtypeStruct((height, width), F32),
            jax.ShapeDtypeStruct((2, groups, part, channels), BF16),
        ),
        in_specs=[hbm] * 8,
        out_specs=(vmem,) * 2,
        scratch_shapes=[
            pltpu.VMEM((1, rows), jnp.int32),
            pltpu.VMEM((1, rows), jnp.int32),
            pltpu.VMEM((rows, steps), BF16),
            pltpu.VMEM((height, width), F32),
            pltpu.VMEM((3, 3 * steps, channels), BF16),
            pltpu.VMEM((1, channels), F32),
            pltpu.VMEM((3, 3, channels), BF16),
            pltpu.SMEM((1,), F32),
            dma((8,)),
            pltpu.VMEM((tiles, CAP + 8, steps), BF16),
            pltpu.VMEM((tiles, CAP + 8, steps), BF16),
            pltpu.VMEM(((height + 2 * HALO) * width, steps), BF16),
            pltpu.VMEM(((height + 2 * HALO) * width, 3 * steps), BF16),
            pltpu.VMEM((pixels, channels), F32),
            pltpu.VMEM(((height + HALO) * width, channels), BF16),
            pltpu.VMEM((height, width), F32),
            pltpu.VMEM((height, width), F32),
            pltpu.VMEM((24, channels), F32),
            pltpu.VMEM((5, tp, width), F32),
            pltpu.VMEM((24, pixels), F32),
            pltpu.VMEM((2, padded, channels), F32),
            pltpu.VMEM((padded, channels), F32),
            pltpu.VMEM((padded, channels), F32),
            pltpu.VMEM((outer, inner * part, channels), F32),
            pltpu.VMEM((inner, part, channels), F32),
            pltpu.VMEM((2, groups, part, channels), BF16),
            dma((tiles,)), dma((tiles,)),
            dma((2,)), dma((2,)), dma((2,)), dma((2,)),
            dma((outer,)), dma((outer,)), dma((outer,)), dma((outer,)), dma((inner,)), dma((inner,)),
            dma((inner,)), dma((inner,)), dma((outer,)), dma((outer,)), dma((outer,)), dma((outer,)),
        ],
        compiler_params=pltpu.CompilerParams(
            collective_id=0, has_side_effects=True, vmem_limit_bytes=60 * 1024 * 1024
        ),
        name="step",
    )(
        dest_tile.reshape(1, rows), pixel_bin, waves[0], target[0],
        conv_one.reshape(3, 3 * steps, channels), bias_one.reshape(1, channels), conv_two, bias_two,
    )
    pred, one, bias, two = pl.pallas_call(
        finish_kernel,
        out_shape=(
            jax.ShapeDtypeStruct((height, width), F32),
            jax.ShapeDtypeStruct((3, 3, steps, channels), F32),
            jax.ShapeDtypeStruct((1, channels), F32),
            jax.ShapeDtypeStruct((3, 3, channels), F32),
        ),
        in_specs=[vmem] * 2,
        out_specs=(hbm,) * 4,
        scratch_shapes=[
            pltpu.VMEM((2, padded, channels), F32),
            pltpu.VMEM((3, 3, steps, channels), F32),
            pltpu.VMEM((1, channels), F32),
            pltpu.VMEM((3, 3, channels), F32),
            dma((4,)),
        ],
        name="finish",
    )(pred, gathered)
    return pred[None], one, bias[0], two


def solution(mesh):
    placed = (
        P("rep", "tile", None),
        P("rep", "tile", None),
        P("rep", "tile"),
        P("rep", "tile", None),
        P(),
        P(),
        P(),
        P(),
    )
    return jax.shard_map(
        functools.partial(on_device, mesh.shape["tile"], mesh.shape["rep"]),
        mesh=mesh,
        in_specs=placed,
        out_specs=(P("rep", "tile", None), P(), P(), P()),
        check_vma=False,
    )
```
